512 devices in a mesh: seq: 64 (over z_hi, y, core), head: 8 (over x, z_lo).
Axes of the slice: x: 4, y: 8, z: 8 (z_hi: 4, z_lo: 2; z = z_hi * 2 + z_lo), core: 2. Of those that a mesh axis runs over, the one named last changes fastest.
Arguments:
- target: bfloat16 [16384, 2048], P('seq', 'head'), may hold values from -1000 to 1000, as said below
- source: bfloat16 [16384, 2048], P('seq', 'head'), may hold values from -6 to 6
- w_query: bfloat16 [2048, 2048], P('seq', 'head'), may hold values from -0.125 to 0.125
- w_key: bfloat16 [2048, 2048], P('seq', 'head'), may hold values from -0.125 to 0.125
- w_value: bfloat16 [2048, 2048], P('seq', 'head'), may hold values from -0.125 to 0.125
- w_out: bfloat16 [2048, 2048], P('seq', 'head'), may hold values from -0.125 to 0.125
- band_start: int32 [256], P('seq'), may hold values from 0 to 255, as said below
- band_end: int32 [256], P('seq'), may hold values from 1 to 256, as said below
- cotangent: bfloat16 [16384, 2048], P('seq', 'head'), may hold values from -6 to 6
Outputs:
- attended: bfloat16 [16384, 2048], P('seq', 'head')
- grad_target: bfloat16 [16384, 2048], P('seq', 'head')
- grad_source: bfloat16 [16384, 2048], P('seq', 'head')
The draws below stay inside these ranges and needn't reach their ends.
Inputs may be any that keep to these rules, and one draw needn't show every extreme that they name: `target`: activations of order one, at most some rows much larger. band_start and band_end never fall from block to block; band_start[b] >= b - 1, band_start[b] < band_end[b] <= band_start[b] + 3, band_end[b] <= b + 3; some target block has a band of exactly 3 source blocks. `band_end`: see band_start.
All inputs are finite; a program needn't handle non-finite values.
Results may differ from the reference program's by a relative error of at most 0.02.
Values may be sent and summed in bfloat16 or wider, within the bound.
No kernel may reach another device: no remote copies, remote signals or barrier semaphores. Data moves between devices by JAX's collectives and lax.ppermute only.
A program may use at most 64 MiB of HBM per device.

```python
import jax
import jax.numpy as jnp
from jax import lax

D = 2048
HEADS = 16
HEAD_DIM = 128
BLOCK = 64
MAXW = 3
TOK_DEV = 256
TOKENS = 16384
NBLK = 256
N_HEAD = 8


def band_pair(key):
    base = jax.random.fold_in(key, 7)
    first_key, second_key = jax.random.split(base)
    blocks = jnp.arange(NBLK, dtype=jnp.int32)
    lean = jax.random.randint(first_key, (NBLK,), 0, 2).astype(jnp.int32)
    lean = lean.at[NBLK - 1].set(1)
    shard_first = blocks % (TOK_DEV // BLOCK) == 0
    lean = jnp.where(shard_first, 0, lean).astype(jnp.int32)
    start = jnp.maximum(blocks - 1 + lean, 0)
    widths = jax.random.randint(second_key, (NBLK,), 1, MAXW + 1).astype(jnp.int32)
    widths = widths.at[0].set(1).at[NBLK // 2].set(MAXW)
    reach = lax.cummax(start + widths, axis=0)
    finish = jnp.minimum(jnp.minimum(reach, start + MAXW), NBLK)
    return (start.astype(jnp.int32), finish.astype(jnp.int32))


def draw_band_start(key, part):
    return band_pair(key)[0]


def draw_band_end(key, part):
    return band_pair(key)[1]


def draw_target(key, part):
    keys = jax.random.split(jax.random.fold_in(key, 11), 1)
    values = jax.random.truncated_normal(keys[0], -4.0, 4.0, (TOKENS, D), jnp.float32)
    return values.astype(jnp.bfloat16)


def steps_of(key, shape, shards, low, largest):
    loudness, own = 1.0, jax.random.fold_in(key, 6)
    for dim, shards_of in shards:
        heights = jnp.exp(jax.random.uniform(jax.random.fold_in(own, dim), (shards_of,), jnp.float32, low / len(shards), largest / len(shards)))
        loudness = loudness * jnp.repeat(heights, shape[dim] // shards_of).reshape([-1 if axis == dim else 1 for axis in range(len(shape))])
    return loudness


def bell_draw(stream_key, dims, scale, limit, cuts=(), kind=jnp.bfloat16):
    entries = scale * jax.random.normal(stream_key, dims, jnp.float32)
    if cuts:
        entries = entries * steps_of(stream_key, dims, cuts, -0.22, 0.18)
    return jnp.clip(entries, -limit, limit).astype(kind)


def setup_inputs(seed: int = 0) -> dict:
    seeds = jax.random.split(jax.random.key(seed), 10)
    return {
        "target": draw_target(jax.random.fold_in(seeds[9], 71), 0),
        "source": bell_draw(seeds[1], (TOKENS, D), 1.0, 6.0, ((0, 64), (1, 8))),
        "w_query": bell_draw(seeds[2], (D, D), D ** -0.5, 0.125, ((0, 64), (1, 8))),
        "w_key": bell_draw(seeds[3], (D, D), D ** -0.5, 0.125, ((0, 64), (1, 8))),
        "w_value": bell_draw(seeds[4], (D, D), D ** -0.5, 0.125, ((0, 64), (1, 8))),
        "w_out": bell_draw(seeds[5], (D, D), D ** -0.5, 0.125, ((0, 64), (1, 8))),
        "band_start": draw_band_start(jax.random.fold_in(seeds[9], 71), 0),
        "band_end": draw_band_end(jax.random.fold_in(seeds[9], 71), 0),
        "cotangent": bell_draw(seeds[8], (TOKENS, D), 1.0, 6.0, ((0, 64), (1, 8))),
    }


def group_sum(pairs):
    width = D // N_HEAD
    rows = pairs[0][0].shape[0]
    total = jnp.zeros((rows, D), jnp.float32)
    for group in range(N_HEAD):
        part = jnp.zeros((rows, D), jnp.float32)
        for left, right in pairs:
            part = part + lax.dot_general(left[:, group * width:(group + 1) * width], right[:, group * width:(group + 1) * width], (((1,), (1,)), ((), ())), preferred_element_type=jnp.float32)
        part = lax.optimization_barrier(part.astype(jnp.bfloat16))
        total = total + part.astype(jnp.float32)
    return total


def reference(target, source, w_query, w_key, w_value, w_out, band_start, band_end, cotangent):
    fone = jnp.float32
    half = jnp.bfloat16
    query = jnp.dot(target, w_query, preferred_element_type=fone).astype(half)
    key = jnp.dot(source, w_key, preferred_element_type=fone).astype(half)
    value = jnp.dot(source, w_value, preferred_element_type=fone).astype(half)
    span = MAXW * BLOCK
    first = jnp.clip(band_start * BLOCK, 0, TOKENS - span).astype(jnp.int32)
    rows_idx = first[:, None] + jnp.arange(span, dtype=jnp.int32)[None, :]
    key_block = rows_idx // BLOCK
    visible = (key_block >= band_start[:, None]) & (key_block < band_end[:, None])
    q_blocks = query.reshape(NBLK, BLOCK, HEADS, HEAD_DIM).astype(fone)
    k_blocks = key[rows_idx].reshape(NBLK, span, HEADS, HEAD_DIM).astype(fone)
    v_blocks = value[rows_idx].reshape(NBLK, span, HEADS, HEAD_DIM).astype(fone)
    scale = HEAD_DIM ** -0.5
    scores = jnp.einsum("nqhe,nkhe->nhqk", q_blocks, k_blocks) * scale
    scores = jnp.where(visible[:, None, None, :], scores, -jnp.inf)
    top = jnp.max(scores, axis=-1, keepdims=True)
    expo = jnp.exp(scores - top)
    prob = expo / jnp.sum(expo, axis=-1, keepdims=True)
    prob_b = lax.optimization_barrier(prob.astype(half)).astype(fone)
    context = jnp.einsum("nhqk,nkhe->nqhe", prob_b, v_blocks).astype(half)
    attended = group_sum([(context.reshape(TOKENS, D), w_out)]).astype(half)
    d_context = jnp.dot(cotangent, w_out, preferred_element_type=fone).astype(half)
    dc_blocks = d_context.reshape(NBLK, BLOCK, HEADS, HEAD_DIM).astype(fone)
    delta = jnp.sum(dc_blocks * context.astype(fone), axis=-1)
    delta = jnp.transpose(delta, (0, 2, 1))[..., None]
    d_prob = jnp.einsum("nqhe,nkhe->nhqk", dc_blocks, v_blocks)
    d_score = (prob * (d_prob - delta) * scale).astype(half)
    d_score = lax.optimization_barrier(d_score).astype(fone)
    d_query = jnp.einsum("nhqk,nkhe->nqhe", d_score, k_blocks).astype(half)
    dk_blocks = jnp.einsum("nhqk,nqhe->nkhe", d_score, q_blocks)
    dv_blocks = jnp.einsum("nhqk,nqhe->nkhe", prob_b, dc_blocks)
    flat = rows_idx.reshape(-1)
    d_key = jnp.zeros((TOKENS, D), fone).at[flat].add(dk_blocks.reshape(-1, D)).astype(half)
    d_value = jnp.zeros((TOKENS, D), fone).at[flat].add(dv_blocks.reshape(-1, D)).astype(half)
    grad_target = group_sum([(d_query.reshape(TOKENS, D), w_query)]).astype(half)
    grad_source = group_sum([(d_key, w_key), (d_value, w_value)]).astype(half)
    return (attended, grad_target, grad_source)
```

```python
import jax
import jax.numpy as jnp
from jax import lax
from jax.sharding import PartitionSpec as P

HEAD_DIM = 128
BLOCK = 64
MAXW = 3
N_Z, N_Y, N_CORE = 4, 8, 2


Z_GROUPS = [[(z * N_Y + y) * N_CORE + c for z in range(N_Z)] for y in range(N_Y) for c in range(N_CORE)]
Y_GROUPS = [[(z * N_Y + y) * N_CORE + c for y in range(N_Y)] for z in range(N_Z) for c in range(N_CORE)]


def passed_along(shard, axis, by):
    count = lax.axis_size(axis)
    pairs = [(i, i + by) for i in range(count) if 0 <= i + by < count]
    return lax.ppermute(shard, axis, pairs)


def dot(left, right):
    return jnp.dot(left, right, preferred_element_type=jnp.float32)


def times_transpose(left, right):
    return lax.dot_general(
        left, right, (((1,), (1,)), ((), ())), preferred_element_type=jnp.float32
    )


def per_device(target, source, w_query, w_key, w_value, w_out, band_start, band_end, cotangent):
    fone = jnp.float32
    half = jnp.bfloat16
    rows = target.shape[0]
    width = w_query.shape[1]
    heads = width // HEAD_DIM
    blocks = rows // BLOCK
    right_rows = (MAXW - 1) * BLOCK
    scale = HEAD_DIM ** (-0.5)
    n_head = lax.axis_size("head")
    n_seq = lax.axis_size("seq")
    shard = lax.axis_index("seq")

    w_mine = jnp.stack([w_query, w_key, w_value, w_out])
    w_z = lax.all_gather(w_mine, "seq", axis=0, axis_index_groups=Z_GROUPS)
    acts = jnp.stack([target, source, cotangent])
    acts, w_z = lax.optimization_barrier((acts, w_z))
    w_y = lax.all_gather(w_z, "seq", axis=0, axis_index_groups=Y_GROUPS)
    acts = jnp.broadcast_to(acts[None], (n_head,) + acts.shape)
    acts = lax.all_to_all(acts, "head", 0, 0)
    acts, w_y = lax.optimization_barrier((acts, w_y))
    w_other = lax.ppermute(w_y, "seq", [(i, i ^ 1) for i in range(n_seq)])
    first = shard % 2 == 0
    both = jnp.stack([jnp.where(first, w_y, w_other), jnp.where(first, w_other, w_y)])
    weights = jnp.transpose(both, (3, 2, 1, 0, 4, 5)).reshape(4, -1, width)
    wq, wk, wv, wo = (weights[i] for i in range(4))
    acts = jnp.transpose(acts, (1, 2, 0, 3)).reshape(3, rows, -1)

    packed = jnp.concatenate([dot(acts[1], wk).astype(half), dot(acts[1], wv).astype(half)], 1)
    from_prev = passed_along(packed[rows - BLOCK :], "seq", 1)
    from_next = passed_along(packed[:right_rows], "seq", -1)
    query = dot(acts[0], wq).astype(half)
    d_context = dot(acts[2], wo).astype(half)
    window = jnp.concatenate([from_prev, packed, from_next], 0)
    span_all = window.shape[0]
    anchor = shard * blocks - 1
    low = band_start - anchor
    high = band_end - anchor
    q_heads = query.reshape(rows, heads, HEAD_DIM)
    kv_heads = window.reshape(span_all, 2 * heads, HEAD_DIM)
    key_block = jnp.arange(span_all, dtype=jnp.int32) // BLOCK
    low_rows = jnp.repeat(low, BLOCK)
    high_rows = jnp.repeat(high, BLOCK)
    k_heads = kv_heads[:, :heads]
    v_heads = kv_heads[:, heads:]
    visible = (key_block[None, :] >= low_rows[:, None]) & (key_block[None, :] < high_rows[:, None])
    scores = jnp.einsum("qhe,khe->hqk", q_heads, k_heads, preferred_element_type=fone) * scale
    scores = jnp.where(visible[None], scores, -jnp.inf)
    top = jnp.max(scores, axis=-1, keepdims=True)
    expo = jnp.exp(scores - top)
    prob = expo / jnp.sum(expo, axis=-1, keepdims=True)
    prob_b = prob.astype(half)
    context = jnp.einsum("hqk,khe->qhe", prob_b, v_heads, preferred_element_type=fone).astype(half)
    dc_heads = d_context.reshape(context.shape)
    delta = jnp.sum(dc_heads.astype(fone) * context.astype(fone), axis=-1)
    delta = jnp.transpose(delta, (1, 0))[..., None]
    d_prob = jnp.einsum("qhe,khe->hqk", dc_heads, v_heads, preferred_element_type=fone)
    d_score = (prob * (d_prob - delta) * scale).astype(half)
    dk = jnp.einsum("hqk,qhe->khe", d_score, q_heads, preferred_element_type=fone)
    dv = jnp.einsum("hqk,qhe->khe", prob_b, dc_heads, preferred_element_type=fone)
    dkv = jnp.concatenate([dk.reshape(span_all, width), dv.reshape(span_all, width)], 1)
    back_next = passed_along(dkv[:BLOCK], "seq", -1)
    back_prev = passed_along(dkv[BLOCK + rows :], "seq", 1)
    attended = times_transpose(context.reshape(rows, width), wo).astype(half)
    d_query = jnp.einsum("hqk,khe->qhe", d_score, k_heads, preferred_element_type=fone).astype(half)
    grad_target = times_transpose(d_query.reshape(rows, width), wq).astype(half)
    owned = dkv[BLOCK : BLOCK + rows]
    owned = owned.at[rows - BLOCK :].add(back_next)
    owned = owned.at[:right_rows].add(back_prev)
    d_key = owned[:, :width].astype(half)
    d_value = owned[:, width:].astype(half)
    grad_source = (times_transpose(d_key, wk) + times_transpose(d_value, wv)).astype(half)

    terms = jnp.stack([attended, grad_target, grad_source])
    terms = jnp.transpose(terms.reshape(3, rows, n_head, width), (2, 0, 1, 3))
    terms = lax.all_to_all(terms, "head", 0, 0)
    outs = jnp.sum(terms.astype(fone), axis=0).astype(half)
    return (outs[0], outs[1], outs[2])


def solution(mesh):
    sharded = P("seq", "head")
    in_specs = (sharded,) * 6 + (P("seq"), P("seq"), sharded)
    return jax.shard_map(
        per_device, mesh=mesh, in_specs=in_specs, out_specs=(sharded,) * 3, check_vma=False
    )
```

```python
import jax
import jax.numpy as jnp
from jax import lax
from jax.sharding import PartitionSpec as P

HEAD_DIM = 128
BLOCK = 64
MAXW = 3
N_Z, N_Y, N_CORE = 4, 8, 2


Z_GROUPS = [[(z * N_Y + y) * N_CORE + c for z in range(N_Z)] for y in range(N_Y) for c in range(N_CORE)]
Y_GROUPS = [[(z * N_Y + y) * N_CORE + c for y in range(N_Y)] for z in range(N_Z) for c in range(N_CORE)]


def passed_along(shard, axis, by):
    count = lax.axis_size(axis)
    pairs = [(i, i + by) for i in range(count) if 0 <= i + by < count]
    return lax.ppermute(shard, axis, pairs)


def dot(left, right):
    return jnp.dot(left, right, preferred_element_type=jnp.float32)


def times_transpose(left, right):
    return lax.dot_general(
        left, right, (((1,), (1,)), ((), ())), preferred_element_type=jnp.float32
    )


def per_device(target, source, w_query, w_key, w_value, w_out, band_start, band_end, cotangent):
    fone = jnp.float32
    half = jnp.bfloat16
    rows = target.shape[0]
    width = w_query.shape[1]
    heads = width // HEAD_DIM
    blocks = rows // BLOCK
    right_rows = (MAXW - 1) * BLOCK
    scale = HEAD_DIM ** (-0.5)
    n_head = lax.axis_size("head")
    n_seq = lax.axis_size("seq")
    shard = lax.axis_index("seq")

    w_mine = jnp.stack([w_query, w_key, w_value, w_out])
    w_z = lax.all_gather(w_mine, "seq", axis=0, axis_index_groups=Z_GROUPS)
    acts = jnp.stack([target, source, cotangent])
    acts, w_z = lax.optimization_barrier((acts, w_z))
    w_y = lax.all_gather(w_z, "seq", axis=0, axis_index_groups=Y_GROUPS)
    acts = jnp.broadcast_to(acts[None], (n_head,) + acts.shape)
    acts = lax.all_to_all(acts, "head", 0, 0)
    acts, w_y = lax.optimization_barrier((acts, w_y))
    w_other = lax.ppermute(w_y, "seq", [(i, i ^ 1) for i in range(n_seq)])
    first = shard % 2 == 0
    both = jnp.stack([jnp.where(first, w_y, w_other), jnp.where(first, w_other, w_y)])
    weights = jnp.transpose(both, (3, 2, 1, 0, 4, 5)).reshape(4, -1, width)
    wq, wk, wv, wo = (weights[i] for i in range(4))
    acts = jnp.transpose(acts, (1, 2, 0, 3)).reshape(3, rows, -1)

    packed = jnp.concatenate([dot(acts[1], wk).astype(half), dot(acts[1], wv).astype(half)], 1)
    from_prev = passed_along(packed[rows - BLOCK :], "seq", 1)
    from_next = passed_along(packed[:right_rows], "seq", -1)
    query = dot(acts[0], wq).astype(half)
    d_context = dot(acts[2], wo).astype(half)
    window = jnp.concatenate([from_prev, packed, from_next], 0)
    span_all = window.shape[0]
    anchor = shard * blocks - 1
    low = band_start - anchor
    high = band_end - anchor
    q_heads = query.reshape(rows, heads, HEAD_DIM)
    kv_heads = window.reshape(span_all, 2 * heads, HEAD_DIM)
    key_block = jnp.arange(span_all, dtype=jnp.int32) // BLOCK
    low_rows = jnp.repeat(low, BLOCK)
    high_rows = jnp.repeat(high, BLOCK)
    k_heads = kv_heads[:, :heads]
    v_heads = kv_heads[:, heads:]
    visible = (key_block[None, :] >= low_rows[:, None]) & (key_block[None, :] < high_rows[:, None])
    scores = jnp.einsum("qhe,khe->hqk", q_heads, k_heads, preferred_element_type=fone) * scale
    scores = jnp.where(visible[None], scores, -jnp.inf)
    top = jnp.max(scores, axis=-1, keepdims=True)
    expo = jnp.exp(scores - top)
    prob = expo / jnp.sum(expo, axis=-1, keepdims=True)
    prob_b = prob.astype(half)
    context = jnp.einsum("hqk,khe->qhe", prob_b, v_heads, preferred_element_type=fone).astype(half)
    dc_heads = d_context.reshape(context.shape)
    delta = jnp.sum(dc_heads.astype(fone) * context.astype(fone), axis=-1)
    delta = jnp.transpose(delta, (1, 0))[..., None]
    d_prob = jnp.einsum("qhe,khe->hqk", dc_heads, v_heads, preferred_element_type=fone)
    d_score = (prob * (d_prob - delta) * scale).astype(half)
    dk = jnp.einsum("hqk,qhe->khe", d_score, q_heads, preferred_element_type=fone)
    dv = jnp.einsum("hqk,qhe->khe", prob_b, dc_heads, preferred_element_type=fone)
    dkv = jnp.concatenate([dk.reshape(span_all, width), dv.reshape(span_all, width)], 1)
    back_next = passed_along(dkv[:BLOCK], "seq", -1)
    back_prev = passed_along(dkv[BLOCK + rows :], "seq", 1)
    attended = times_transpose(context.reshape(rows, width), wo).astype(half)
    attended = jnp.transpose(attended.reshape(rows, n_head, width), (1, 0, 2))
    attended = lax.all_to_all(attended, "head", 0, 0)
    attended = jnp.sum(attended.astype(fone), axis=0).astype(half)
    d_query = jnp.einsum("hqk,khe->qhe", d_score, k_heads, preferred_element_type=fone).astype(half)
    grad_target = times_transpose(d_query.reshape(rows, width), wq).astype(half)
    owned = dkv[BLOCK : BLOCK + rows]
    owned = owned.at[rows - BLOCK :].add(back_next)
    owned = owned.at[:right_rows].add(back_prev)
    d_key = owned[:, :width].astype(half)
    d_value = owned[:, width:].astype(half)
    grad_source = (times_transpose(d_key, wk) + times_transpose(d_value, wv)).astype(half)

    terms = jnp.stack([grad_target, grad_source])
    terms = jnp.transpose(terms.reshape(2, rows, n_head, width), (2, 0, 1, 3))
    terms = lax.all_to_all(terms, "head", 0, 0)
    outs = jnp.sum(terms.astype(fone), axis=0).astype(half)
    return (attended, outs[0], outs[1])


def solution(mesh):
    sharded = P("seq", "head")
    in_specs = (sharded,) * 6 + (P("seq"), P("seq"), sharded)
    return jax.shard_map(
        per_device, mesh=mesh, in_specs=in_specs, out_specs=(sharded,) * 3, check_vma=False
    )
```

```python
import jax
import jax.numpy as jnp
from jax import lax
from jax.experimental import pallas as pl
from jax.experimental.pallas import tpu as pltpu
from jax.sharding import PartitionSpec as P

HEAD_DIM = 128
BLOCK = 64
MAXW = 3
N_Z, N_Y, N_CORE = 4, 8, 2
N_SEQ = N_Z * N_Y * N_CORE
N_HEAD = 8
ROWS = 256
WIDTH = 256
SHARD = 32
PAIR = 2 * BLOCK
REACH = 3 * PAIR
HALF = jnp.bfloat16
FONE = jnp.float32


Y_GROUPS = [
    [(z * N_Y + y) * N_CORE + c for y in range(N_Y)] for z in range(N_Z) for c in range(N_CORE)
]


def passed_along(shard, axis, by):
    pairs = [(i, i + by) for i in range(N_SEQ) if 0 <= i + by < N_SEQ]
    return lax.ppermute(shard, axis, pairs)


def from_z(shard, by):
    step = N_Y * N_CORE
    return lax.ppermute(shard, "seq", [(i, (i - by * step) % N_SEQ) for i in range(N_SEQ)])


def nt(left, right):
    return lax.dot_general(left, right, (((1,), (1,)), ((), ())), preferred_element_type=FONE)


def tn(left, right):
    return lax.dot_general(left, right, (((0,), (0,)), ((), ())), preferred_element_type=FONE)


def fetch_weights(place, mine, other, whole, sems):
    core = place[1]
    for head in range(N_HEAD):
        behind = (head // 2 - place[0]) & (N_Z - 1)
        for step in range(4):
            y = 4 * (head % 2) + step
            row = head * WIDTH + step * 2 * SHARD
            for ref, side in ((mine, core), (other, 1 - core)):
                at = pl.multiple_of(row + side * SHARD, SHARD)
                pltpu.make_async_copy(
                    ref.at[y, behind], whole.at[:, pl.ds(at, SHARD), :], sems.at[head]
                ).start()


def await_weights(whole, sems):
    for head in range(N_HEAD):
        part = whole.at[:, pl.ds(head * WIDTH, WIDTH), :]
        pltpu.make_async_copy(part, part, sems.at[head]).wait()


def project(place, acts, mine, other, band, kv, qd, to_next, to_prev, whole, sems):
    fetch_weights(place, mine, other, whole, sems)
    lefts = [
        jnp.concatenate([acts[head, which] for head in range(N_HEAD)], axis=1) for which in range(3)
    ]
    await_weights(whole, sems)

    def product(which, weight):
        return jnp.dot(lefts[which], whole[weight], preferred_element_type=FONE).astype(HALF)

    kv[:, :WIDTH] = product(1, 1)
    kv[:, WIDTH:] = product(1, 2)
    qd[:, :WIDTH] = product(0, 0)
    qd[:, WIDTH:] = product(2, 3)
    to_next[: 3 * BLOCK] = kv[BLOCK:]
    to_next[3 * BLOCK : 5 * BLOCK] = qd[2 * BLOCK :]
    to_next[5 * BLOCK :] = band[...]
    to_prev[: 3 * BLOCK] = kv[: 3 * BLOCK]
    to_prev[3 * BLOCK : 4 * BLOCK] = qd[:BLOCK]
    to_prev[4 * BLOCK :] = band[...]


def attend(place, kv, qd, prev, after, band, mine, other, terms, kvw, qdw, ctx, dq, dkv, whole, sems):
    fetch_weights(place, mine, other, whole, sems)
    kvw[:BLOCK] = jnp.zeros((BLOCK, 2 * WIDTH), HALF)
    kvw[BLOCK : 4 * BLOCK] = prev[: 3 * BLOCK]
    kvw[4 * BLOCK : 8 * BLOCK] = kv[...]
    kvw[8 * BLOCK : 11 * BLOCK] = after[: 3 * BLOCK]
    kvw[11 * BLOCK :] = jnp.zeros((BLOCK, 2 * WIDTH), HALF)
    qdw[: 2 * BLOCK] = prev[3 * BLOCK : 5 * BLOCK]
    qdw[2 * BLOCK : 6 * BLOCK] = qd[...]
    qdw[6 * BLOCK : 7 * BLOCK] = after[3 * BLOCK : 4 * BLOCK]
    qdw[7 * BLOCK :] = jnp.zeros((BLOCK, 2 * WIDTH), HALF)

    own = band[...].astype(FONE)[:, :REACH]
    back = prev[5 * BLOCK :].astype(FONE)[:, :REACH]
    ahead = after[4 * BLOCK :].astype(FONE)[:, :REACH]
    rows = [(back, 2), (back, 3), (own, 0), (own, 1), (own, 2), (own, 3), (ahead, 0), (own, 8)]
    lows = [source[i : i + 1] for source, i in rows]
    highs = [source[i + 4 : i + 5] for source, i in rows]
    lower = lax.broadcasted_iota(jnp.int32, (PAIR, REACH), 0) // BLOCK
    offset = lax.broadcasted_iota(jnp.int32, (PAIR, REACH), 1) // BLOCK - lower - 1
    offset = offset.astype(FONE)
    scale = HEAD_DIM**-0.5
    for head in range(2):
        left = slice(head * HEAD_DIM, (head + 1) * HEAD_DIM)
        right = slice(WIDTH + head * HEAD_DIM, WIDTH + (head + 1) * HEAD_DIM)
        d_key = [None, None]
        d_value = [None, None]
        for pair in range(4):
            low = jnp.where(lower == 0, lows[2 * pair], lows[2 * pair + 1])
            high = jnp.where(lower == 0, highs[2 * pair], highs[2 * pair + 1])
            visible = (offset >= low) & (offset < high)
            here = slice(pair * PAIR, (pair + 1) * PAIR)
            there = slice(pair * PAIR, pair * PAIR + REACH)
            query, d_context = qdw[here, left], qdw[here, right]
            key, value = kvw[there, left], kvw[there, right]
            score = jnp.where(visible, nt(query, key) * scale, -jnp.inf)
            top = jnp.max(score, axis=-1, keepdims=True)
            expo = jnp.where(visible, jnp.exp(score - top), 0.0)
            prob = expo / jnp.maximum(jnp.sum(expo, axis=-1, keepdims=True), 0.5)
            prob_b = prob.astype(HALF)
            context = jnp.dot(prob_b, value, preferred_element_type=FONE).astype(HALF)
            delta = jnp.sum(
                d_context.astype(FONE) * context.astype(FONE), axis=-1, keepdims=True
            )
            d_prob = nt(d_context, value)
            d_score = (prob * (d_prob - delta) * scale).astype(HALF)
            if pair in (1, 2):
                mine_rows = slice((pair - 1) * PAIR, pair * PAIR)
                ctx[mine_rows, left] = context
                dq[mine_rows, left] = jnp.dot(d_score, key, preferred_element_type=FONE).astype(HALF)
            for part in range(2):
                column = 2 + part - pair
                if 0 <= column < 3:
                    cut = slice(column * PAIR, (column + 1) * PAIR)
                    k_term = tn(d_score[:, cut], query)
                    v_term = tn(prob_b[:, cut], d_context)
                    first = d_key[part] is None
                    d_key[part] = k_term if first else d_key[part] + k_term
                    d_value[part] = v_term if first else d_value[part] + v_term
        for part in range(2):
            cut = slice(part * PAIR, (part + 1) * PAIR)
            dkv[cut, left] = d_key[part].astype(HALF)
            dkv[cut, right] = d_value[part].astype(HALF)

    await_weights(whole, sems)
    for head in range(N_HEAD):
        cut = slice(head * WIDTH, (head + 1) * WIDTH)
        terms[head, 0] = nt(ctx[...], whole[3, cut]).astype(HALF)
        terms[head, 1] = nt(dq[...], whole[0, cut]).astype(HALF)
        source_term = nt(dkv[:, :WIDTH], whole[1, cut]) + nt(dkv[:, WIDTH:], whole[2, cut])
        terms[head, 2] = source_term.astype(HALF)


SMEM = pl.BlockSpec(memory_space=pltpu.SMEM)
VMEM = pl.BlockSpec(memory_space=pltpu.VMEM)
ANY = pl.BlockSpec(memory_space=pl.ANY)


def shaped(*dims):
    return jax.ShapeDtypeStruct(dims, HALF)


def weight_scratch():
    return [
        pltpu.VMEM((4, N_SEQ * SHARD, WIDTH), HALF),
        pltpu.SemaphoreType.DMA((N_HEAD,)),
    ]


def call_project(place, acts, mine, other, band):
    return pl.pallas_call(
        project,
        name="project",
        out_shape=(
            shaped(ROWS, 2 * WIDTH),
            shaped(ROWS, 2 * WIDTH),
            shaped(5 * BLOCK + 16, 2 * WIDTH),
            shaped(4 * BLOCK + 16, 2 * WIDTH),
        ),
        in_specs=[SMEM, VMEM, ANY, ANY, VMEM],
        out_specs=(VMEM,) * 4,
        scratch_shapes=weight_scratch(),
    )(place, acts, mine, other, band)


def call_attend(place, kv, qd, prev, after, band, mine, other):
    return pl.pallas_call(
        attend,
        name="attend",
        out_shape=shaped(N_HEAD, 3, ROWS, WIDTH),
        in_specs=[SMEM, VMEM, VMEM, VMEM, VMEM, VMEM, ANY, ANY],
        out_specs=VMEM,
        scratch_shapes=[
            pltpu.VMEM((12 * BLOCK, 2 * WIDTH), HALF),
            pltpu.VMEM((8 * BLOCK, 2 * WIDTH), HALF),
            pltpu.VMEM((ROWS, WIDTH), HALF),
            pltpu.VMEM((ROWS, WIDTH), HALF),
            pltpu.VMEM((ROWS, 2 * WIDTH), HALF),
            *weight_scratch(),
        ],
    )(place, kv, qd, prev, after, band, mine, other)


def band_rows(band_start, band_end, shard):
    blocks = ROWS // BLOCK
    before = shard * blocks + jnp.arange(blocks, dtype=jnp.int32) - 1
    spare = jnp.zeros((8,), jnp.int32)
    offsets = jnp.concatenate([band_start - before, band_end - before, spare]).astype(HALF)
    return jnp.broadcast_to(offsets[:, None], (16, 2 * WIDTH))


def per_device(target, source, w_query, w_key, w_value, w_out, band_start, band_end, cotangent):
    shard = lax.axis_index("seq")
    place = jnp.stack([shard // (N_Y * N_CORE), shard % N_CORE]).astype(jnp.int32)
    band = band_rows(band_start, band_end, shard)

    w_mine = jnp.stack([w_query, w_key, w_value, w_out])
    w_z = jnp.stack([w_mine] + [from_z(w_mine, by) for by in range(1, N_Z)])
    acts = jnp.stack([target, source, cotangent])
    acts = jnp.broadcast_to(acts[None], (N_HEAD,) + acts.shape)
    acts, w_z = lax.optimization_barrier((acts, w_z))
    w_y = lax.all_gather(w_z, "seq", axis=0, axis_index_groups=Y_GROUPS)
    acts = lax.all_to_all(acts, "head", 0, 0)
    acts, w_y = lax.optimization_barrier((acts, w_y))
    w_other = lax.ppermute(w_y, "seq", [(i, i ^ 1) for i in range(N_SEQ)])

    kv, qd, to_next, to_prev = call_project(place, acts, w_y, w_other, band)
    prev = passed_along(to_next, "seq", 1)
    after = passed_along(to_prev, "seq", -1)
    terms = call_attend(place, kv, qd, prev, after, band, w_y, w_other)
    terms = lax.all_to_all(terms, "head", 0, 0)
    return tuple(
        jnp.sum(terms[:, i].astype(FONE), axis=0).astype(HALF) for i in range(3)
    )


def solution(mesh):
    sharded = P("seq", "head")
    in_specs = (sharded,) * 6 + (P("seq"), P("seq"), sharded)
    return jax.shard_map(
        per_device, mesh=mesh, in_specs=in_specs, out_specs=(sharded,) * 3, check_vma=False
    )
```

```python
import jax
import jax.numpy as jnp
from jax import lax
from jax.experimental import pallas as pl
from jax.experimental.pallas import tpu as pltpu
from jax.sharding import PartitionSpec as P


HEAD_DIM = 128
BLOCK = 64
N_Z, N_Y, N_CORE = 4, 8, 2
N_SEQ = N_Z * N_Y * N_CORE
N_HEAD = 8
ROWS = 256
WIDTH = 256
SHARD = 32
PAIR = 2 * BLOCK
REACH = 3 * PAIR
HALF = jnp.bfloat16
FONE = jnp.float32


YC_GROUPS = [[z * N_Y * N_CORE + k for k in range(N_Y * N_CORE)] for z in range(N_Z)]


def passed_along(shard, axis, by):
    pairs = [(i, i + by) for i in range(N_SEQ) if 0 <= i + by < N_SEQ]
    return lax.ppermute(shard, axis, pairs)


def from_z(shard, by):
    step = N_Y * N_CORE
    return lax.ppermute(shard, "seq", [(i, (i - by * step) % N_SEQ) for i in range(N_SEQ)])


def nt(left, right):
    return lax.dot_general(left, right, (((1,), (1,)), ((), ())), preferred_element_type=FONE)


def tn(left, right):
    return lax.dot_general(left, right, (((0,), (0,)), ((), ())), preferred_element_type=FONE)


def fetch_weights(place, gathered, which, whole, sem):
    per = N_SEQ // N_HEAD
    for slot, weight in enumerate(which):
        for head in range(N_HEAD):
            behind = (head // 2 - place[0]) & (N_Z - 1)
            pltpu.make_async_copy(
                gathered.at[pl.ds(per * (head % 2), per), behind, weight],
                whole.at[slot, pl.ds(per * head, per)],
                sem.at[slot],
            ).start()


def await_copies(ref, sem, slot):
    pltpu.make_async_copy(ref.at[slot], ref.at[slot], sem.at[slot]).wait()


def fetch_acts(acts, which, left, sem):
    for slot, act in enumerate(which):
        for head in range(N_HEAD):
            pltpu.make_async_copy(
                acts.at[head, act], left.at[slot, :, pl.ds(head * WIDTH, WIDTH)], sem.at[slot]
            ).start()


def whole_rows(whole, slot):
    return whole[slot].reshape(N_SEQ * SHARD, WIDTH)


def piece(whole, slot, head):
    per = N_SEQ // N_HEAD
    return whole[slot, per * head : per * (head + 1)].reshape(WIDTH, WIDTH)


def project_kv(place, acts, gathered, band, kv, to_next, to_prev, whole, left, w_sem, a_sem):
    fetch_acts(acts, (1,), left, a_sem)
    fetch_weights(place, gathered, (1, 2), whole, w_sem)
    await_copies(left, a_sem, 0)
    for slot in range(2):
        await_copies(whole, w_sem, slot)
        cut = slice(slot * WIDTH, (slot + 1) * WIDTH)
        kv[:, cut] = jnp.dot(
            left[0], whole_rows(whole, slot), preferred_element_type=FONE
        ).astype(HALF)
    to_next[: 3 * BLOCK] = kv[BLOCK:]
    to_next[3 * BLOCK :] = band[...]
    to_prev[: 3 * BLOCK] = kv[: 3 * BLOCK]
    to_prev[3 * BLOCK :] = band[...]


def project_qd(place, acts, gathered, qd, to_next, to_prev, whole, left, w_sem, a_sem):
    fetch_acts(acts, (0, 2), left, a_sem)
    fetch_weights(place, gathered, (0, 3), whole, w_sem)
    for slot in range(2):
        await_copies(left, a_sem, slot)
        await_copies(whole, w_sem, slot)
        cut = slice(slot * WIDTH, (slot + 1) * WIDTH)
        qd[:, cut] = jnp.dot(
            left[slot], whole_rows(whole, slot), preferred_element_type=FONE
        ).astype(HALF)
    to_next[...] = qd[2 * BLOCK :]
    to_prev[...] = qd[:BLOCK]


def fill_keys(kvw, kv, prev, after):
    kvw[:BLOCK] = jnp.zeros((BLOCK, 2 * WIDTH), HALF)
    kvw[BLOCK : 4 * BLOCK] = prev[: 3 * BLOCK]
    kvw[4 * BLOCK : 8 * BLOCK] = kv[...]
    kvw[8 * BLOCK : 11 * BLOCK] = after[: 3 * BLOCK]
    kvw[11 * BLOCK :] = jnp.zeros((BLOCK, 2 * WIDTH), HALF)


def masks(prev, after, band):
    own = band[...].astype(FONE)[:, :REACH]
    back = prev[3 * BLOCK :].astype(FONE)[:, :REACH]
    ahead = after[3 * BLOCK :].astype(FONE)[:, :REACH]
    rows = [(back, 2), (back, 3), (own, 0), (own, 1), (own, 2), (own, 3), (ahead, 0), (own, 8)]
    lows = [source[i : i + 1] for source, i in rows]
    highs = [source[i + 4 : i + 5] for source, i in rows]
    lower = lax.broadcasted_iota(jnp.int32, (PAIR, REACH), 0) // BLOCK
    offset = lax.broadcasted_iota(jnp.int32, (PAIR, REACH), 1) // BLOCK - lower - 1
    offset = offset.astype(FONE)

    def visible(pair):
        low = jnp.where(lower == 0, lows[2 * pair], lows[2 * pair + 1])
        high = jnp.where(lower == 0, highs[2 * pair], highs[2 * pair + 1])
        return (offset >= low) & (offset < high)

    return visible


def softmax(query, key, visible):
    score = jnp.where(visible, nt(query, key) * HEAD_DIM**-0.5, -jnp.inf)
    top = jnp.max(score, axis=-1, keepdims=True)
    expo = jnp.where(visible, jnp.exp(score - top), 0.0)
    return expo / jnp.maximum(jnp.sum(expo, axis=-1, keepdims=True), 0.5)


def columns_of(head):
    low = head * HEAD_DIM
    return slice(low, low + HEAD_DIM), slice(WIDTH + low, WIDTH + low + HEAD_DIM)


def forward(place, kv, qd, prev, after, band, gathered, terms, kvw, ctx, whole, w_sem):
    fetch_weights(place, gathered, (3,), whole, w_sem)
    fill_keys(kvw, kv, prev, after)
    visible = masks(prev, after, band)
    for pair in (1, 2):
        seen = visible(pair)
        rows = slice((pair - 1) * PAIR, pair * PAIR)
        there = slice(pair * PAIR, pair * PAIR + REACH)
        for head in range(2):
            left, right = columns_of(head)
            prob_b = softmax(qd[rows, left], kvw[there, left], seen).astype(HALF)
            context = jnp.dot(prob_b, kvw[there, right], preferred_element_type=FONE)
            ctx[rows, left] = context.astype(HALF)
    await_copies(whole, w_sem, 0)
    for head in range(N_HEAD):
        terms[head] = nt(ctx[...], piece(whole, 0, head)).astype(HALF)


def backward(
    place, kv, qd, prev, after, q_prev, q_after, band, gathered, terms, kvw, qdw, dq, dkv, whole, w_sem
):
    fetch_weights(place, gathered, (0, 1, 2), whole, w_sem)
    fill_keys(kvw, kv, prev, after)
    qdw[: 2 * BLOCK] = q_prev[...]
    qdw[2 * BLOCK : 6 * BLOCK] = qd[...]
    qdw[6 * BLOCK : 7 * BLOCK] = q_after[...]
    qdw[7 * BLOCK :] = jnp.zeros((BLOCK, 2 * WIDTH), HALF)
    visible = masks(prev, after, band)
    for head in range(2):
        left, right = columns_of(head)
        d_key = [None, None]
        d_value = [None, None]
        for pair in range(4):
            here = slice(pair * PAIR, (pair + 1) * PAIR)
            there = slice(pair * PAIR, pair * PAIR + REACH)
            query, d_context = qdw[here, left], qdw[here, right]
            key, value = kvw[there, left], kvw[there, right]
            prob = softmax(query, key, visible(pair))
            prob_b = prob.astype(HALF)
            context = jnp.dot(prob_b, value, preferred_element_type=FONE).astype(HALF)
            delta = jnp.sum(
                d_context.astype(FONE) * context.astype(FONE), axis=-1, keepdims=True
            )
            d_prob = nt(d_context, value)
            d_score = (prob * (d_prob - delta) * HEAD_DIM**-0.5).astype(HALF)
            if pair in (1, 2):
                rows = slice((pair - 1) * PAIR, pair * PAIR)
                dq[rows, left] = jnp.dot(d_score, key, preferred_element_type=FONE).astype(HALF)
            for part in range(2):
                column = 2 + part - pair
                if 0 <= column < 3:
                    cut = slice(column * PAIR, (column + 1) * PAIR)
                    k_term = tn(d_score[:, cut], query)
                    v_term = tn(prob_b[:, cut], d_context)
                    first = d_key[part] is None
                    d_key[part] = k_term if first else d_key[part] + k_term
                    d_value[part] = v_term if first else d_value[part] + v_term
        for part in range(2):
            cut = slice(part * PAIR, (part + 1) * PAIR)
            dkv[cut, left] = d_key[part].astype(HALF)
            dkv[cut, right] = d_value[part].astype(HALF)
    for slot in range(3):
        await_copies(whole, w_sem, slot)
    for head in range(N_HEAD):
        terms[head, 0] = nt(dq[...], piece(whole, 0, head)).astype(HALF)
        source_term = nt(dkv[:, :WIDTH], piece(whole, 1, head)) + nt(
            dkv[:, WIDTH:], piece(whole, 2, head)
        )
        terms[head, 1] = source_term.astype(HALF)


SMEM = pl.BlockSpec(memory_space=pltpu.SMEM)
VMEM = pl.BlockSpec(memory_space=pltpu.VMEM)
ANY = pl.BlockSpec(memory_space=pl.ANY)


def shaped(*dims):
    return jax.ShapeDtypeStruct(dims, HALF)


def scratch(*dims):
    return pltpu.VMEM(dims, HALF)


def matrices(count):
    return scratch(count, N_SEQ, SHARD, WIDTH)


def copies(count):
    return pltpu.SemaphoreType.DMA((count,))


def call_project_kv(place, acts, gathered, band):
    sent = shaped(3 * BLOCK + 16, 2 * WIDTH)
    return pl.pallas_call(
        project_kv,
        name="project_kv",
        out_shape=(shaped(ROWS, 2 * WIDTH), sent, sent),
        in_specs=[SMEM, ANY, ANY, VMEM],
        out_specs=(VMEM,) * 3,
        scratch_shapes=[matrices(2), scratch(1, ROWS, N_HEAD * WIDTH), copies(2), copies(1)],
    )(place, acts, gathered, band)


def call_project_qd(place, acts, gathered):
    return pl.pallas_call(
        project_qd,
        name="project_qd",
        out_shape=(
            shaped(ROWS, 2 * WIDTH),
            shaped(2 * BLOCK, 2 * WIDTH),
            shaped(BLOCK, 2 * WIDTH),
        ),
        in_specs=[SMEM, ANY, ANY],
        out_specs=(VMEM,) * 3,
        scratch_shapes=[matrices(2), scratch(2, ROWS, N_HEAD * WIDTH), copies(2), copies(2)],
    )(place, acts, gathered)


def call_forward(place, kv, qd, prev, after, band, gathered):
    return pl.pallas_call(
        forward,
        name="forward",
        out_shape=shaped(N_HEAD, ROWS, WIDTH),
        in_specs=[SMEM, VMEM, VMEM, VMEM, VMEM, VMEM, ANY],
        out_specs=VMEM,
        scratch_shapes=[
            scratch(12 * BLOCK, 2 * WIDTH),
            scratch(ROWS, WIDTH),
            matrices(1),
            copies(1),
        ],
    )(place, kv, qd, prev, after, band, gathered)


def call_backward(place, kv, qd, prev, after, q_prev, q_after, band, gathered):
    return pl.pallas_call(
        backward,
        name="backward",
        out_shape=shaped(N_HEAD, 2, ROWS, WIDTH),
        in_specs=[SMEM, VMEM, VMEM, VMEM, VMEM, VMEM, VMEM, VMEM, ANY],
        out_specs=VMEM,
        scratch_shapes=[
            scratch(12 * BLOCK, 2 * WIDTH),
            scratch(8 * BLOCK, 2 * WIDTH),
            scratch(ROWS, WIDTH),
            scratch(ROWS, 2 * WIDTH),
            matrices(3),
            copies(3),
        ],
    )(place, kv, qd, prev, after, q_prev, q_after, band, gathered)


def band_rows(band_start, band_end, shard):
    blocks = ROWS // BLOCK
    before = shard * blocks + jnp.arange(blocks, dtype=jnp.int32) - 1
    spare = jnp.zeros((8,), jnp.int32)
    offsets = jnp.concatenate([band_start - before, band_end - before, spare]).astype(HALF)
    return jnp.broadcast_to(offsets[:, None], (16, 2 * WIDTH))


def layer(target, source, w_query, w_key, w_value, w_out, band_start, band_end, cotangent):
    shard = lax.axis_index("seq")
    place = (shard // (N_Y * N_CORE)).astype(jnp.int32)[None]
    band = band_rows(band_start, band_end, shard)

    w_mine = jnp.stack([w_query, w_key, w_value, w_out])
    w_z = jnp.stack([w_mine] + [from_z(w_mine, by) for by in range(1, N_Z)])
    acts = jnp.stack([target, source, cotangent])
    acts = jnp.broadcast_to(acts[None], (N_HEAD,) + acts.shape)
    acts, w_z = lax.optimization_barrier((acts, w_z))
    gathered = lax.all_gather(w_z, "seq", axis=0, axis_index_groups=YC_GROUPS)
    acts = lax.all_to_all(acts, "head", 0, 0)
    acts, gathered, band, place = lax.optimization_barrier((acts, gathered, band, place))

    kv, kv_next, kv_prev = call_project_kv(place, acts, gathered, band)
    prev = passed_along(kv_next, "seq", 1)
    after = passed_along(kv_prev, "seq", -1)
    qd, q_next, q_prev = call_project_qd(place, acts, gathered)
    q_before = passed_along(q_next, "seq", 1)
    q_after = passed_along(q_prev, "seq", -1)
    attended = call_forward(place, kv, qd, prev, after, band, gathered)
    attended = lax.all_to_all(attended, "head", 0, 0)
    attended = jnp.sum(attended.astype(FONE), axis=0).astype(HALF)
    terms = call_backward(place, kv, qd, prev, after, q_before, q_after, band, gathered)
    terms = lax.all_to_all(terms, "head", 0, 0)
    grads = [jnp.sum(terms[:, i].astype(FONE), axis=0).astype(HALF) for i in range(2)]
    return (attended, *grads)


def solution(mesh):
    sharded = P("seq", "head")
    in_specs = (sharded,) * 6 + (P("seq"), P("seq"), sharded)
    return jax.shard_map(
        layer, mesh=mesh, in_specs=in_specs, out_specs=(sharded,) * 3, check_vma=False
    )
```

```python
import jax
import jax.numpy as jnp
from jax import lax
from jax.experimental import pallas as pl
from jax.experimental.pallas import tpu as pltpu
from jax.sharding import PartitionSpec as P

HEAD_DIM = 128
BLOCK = 64
MAXW = 3
N_Z, N_Y, N_CORE = 4, 8, 2
N_SEQ = N_Z * N_Y * N_CORE
N_HEAD = 8
ROWS = 256
WIDTH = 256
SHARD = 32
PAIR = 2 * BLOCK
REACH = 3 * PAIR
HALF = jnp.bfloat16
FONE = jnp.float32


Z_GROUPS = [
    [z * N_Y * N_CORE + k for z in range(N_Z)] for k in range(N_Y * N_CORE)
]
YC_GROUPS = [[z * N_Y * N_CORE + k for k in range(N_Y * N_CORE)] for z in range(N_Z)]


def passed_along(shard, axis, by):
    pairs = [(i, i + by) for i in range(N_SEQ) if 0 <= i + by < N_SEQ]
    return lax.ppermute(shard, axis, pairs)


def nt(left, right):
    return lax.dot_general(left, right, (((1,), (1,)), ((), ())), preferred_element_type=FONE)


def tn(left, right):
    return lax.dot_general(left, right, (((0,), (0,)), ((), ())), preferred_element_type=FONE)


def fetch_weight(gathered, weight, whole, sems):
    per = N_SEQ // N_HEAD
    for head in range(N_HEAD):
        pltpu.make_async_copy(
            gathered.at[pl.ds(per * (head % 2), per), head // 2, weight],
            whole.at[weight, pl.ds(per * head, per)],
            sems.at[weight],
        ).start()


def fetch_acts(acts, which, left, sems):
    for head in range(N_HEAD):
        pltpu.make_async_copy(
            acts.at[head, which], left.at[which, :, pl.ds(head * WIDTH, WIDTH)], sems.at[which]
        ).start()


def await_copies(ref, slot, sems):
    pltpu.make_async_copy(ref.at[slot], ref.at[slot], sems.at[slot]).wait()


def piece(whole, weight, head):
    per = N_SEQ // N_HEAD
    return whole[weight, per * head : per * (head + 1)].reshape(WIDTH, WIDTH)


def project(acts, gathered, band, kv, qd, to_next, to_prev, whole, left, w_sems, a_sems):
    fetch_acts(acts, 1, left, a_sems)
    fetch_weight(gathered, 1, whole, w_sems)
    fetch_weight(gathered, 2, whole, w_sems)
    fetch_acts(acts, 0, left, a_sems)
    fetch_weight(gathered, 0, whole, w_sems)
    fetch_acts(acts, 2, left, a_sems)
    fetch_weight(gathered, 3, whole, w_sems)

    def product(which, weight):
        await_copies(whole, weight, w_sems)
        right = whole[weight].reshape(N_SEQ * SHARD, WIDTH)
        return jnp.dot(left[which], right, preferred_element_type=FONE).astype(HALF)

    await_copies(left, 1, a_sems)
    kv[:, :WIDTH] = product(1, 1)
    kv[:, WIDTH:] = product(1, 2)
    await_copies(left, 0, a_sems)
    qd[:, :WIDTH] = product(0, 0)
    await_copies(left, 2, a_sems)
    qd[:, WIDTH:] = product(2, 3)
    to_next[: 3 * BLOCK] = kv[BLOCK:]
    to_next[3 * BLOCK : 5 * BLOCK] = qd[2 * BLOCK :]
    to_next[5 * BLOCK :] = band[...]
    to_prev[: 3 * BLOCK] = kv[: 3 * BLOCK]
    to_prev[3 * BLOCK : 4 * BLOCK] = qd[:BLOCK]
    to_prev[4 * BLOCK :] = band[...]


def attend(
    kv, qd, prev, after, band, gathered, out, kvw, qdw, ctx, dq, dkv, terms, whole, w_sems, o_sems
):
    for weight in (3, 0, 1, 2):
        fetch_weight(gathered, weight, whole, w_sems)
    kvw[:BLOCK] = jnp.zeros((BLOCK, 2 * WIDTH), HALF)
    kvw[BLOCK : 4 * BLOCK] = prev[: 3 * BLOCK]
    kvw[4 * BLOCK : 8 * BLOCK] = kv[...]
    kvw[8 * BLOCK : 11 * BLOCK] = after[: 3 * BLOCK]
    kvw[11 * BLOCK :] = jnp.zeros((BLOCK, 2 * WIDTH), HALF)
    qdw[: 2 * BLOCK] = prev[3 * BLOCK : 5 * BLOCK]
    qdw[2 * BLOCK : 6 * BLOCK] = qd[...]
    qdw[6 * BLOCK : 7 * BLOCK] = after[3 * BLOCK : 4 * BLOCK]
    qdw[7 * BLOCK :] = jnp.zeros((BLOCK, 2 * WIDTH), HALF)

    own = band[...].astype(FONE)[:, :REACH]
    back = prev[5 * BLOCK :].astype(FONE)[:, :REACH]
    ahead = after[4 * BLOCK :].astype(FONE)[:, :REACH]
    rows = [(back, 2), (back, 3), (own, 0), (own, 1), (own, 2), (own, 3), (ahead, 0), (own, 8)]
    lows = [source[i : i + 1] for source, i in rows]
    highs = [source[i + 4 : i + 5] for source, i in rows]
    lower = lax.broadcasted_iota(jnp.int32, (PAIR, REACH), 0) // BLOCK
    offset = lax.broadcasted_iota(jnp.int32, (PAIR, REACH), 1) // BLOCK - lower - 1
    offset = offset.astype(FONE)
    scale = HEAD_DIM**-0.5
    for head in range(2):
        left = slice(head * HEAD_DIM, (head + 1) * HEAD_DIM)
        right = slice(WIDTH + head * HEAD_DIM, WIDTH + (head + 1) * HEAD_DIM)
        d_key = [None, None]
        d_value = [None, None]
        for pair in range(4):
            low = jnp.where(lower == 0, lows[2 * pair], lows[2 * pair + 1])
            high = jnp.where(lower == 0, highs[2 * pair], highs[2 * pair + 1])
            visible = (offset >= low) & (offset < high)
            here = slice(pair * PAIR, (pair + 1) * PAIR)
            there = slice(pair * PAIR, pair * PAIR + REACH)
            query, d_context = qdw[here, left], qdw[here, right]
            key, value = kvw[there, left], kvw[there, right]
            score = jnp.where(visible, nt(query, key) * scale, -jnp.inf)
            top = jnp.max(score, axis=-1, keepdims=True)
            expo = jnp.where(visible, jnp.exp(score - top), 0.0)
            prob = expo / jnp.maximum(jnp.sum(expo, axis=-1, keepdims=True), 0.5)
            prob_b = prob.astype(HALF)
            context = jnp.dot(prob_b, value, preferred_element_type=FONE).astype(HALF)
            delta = jnp.sum(
                d_context.astype(FONE) * context.astype(FONE), axis=-1, keepdims=True
            )
            d_prob = nt(d_context, value)
            d_score = (prob * (d_prob - delta) * scale).astype(HALF)
            if pair in (1, 2):
                mine_rows = slice((pair - 1) * PAIR, pair * PAIR)
                ctx[mine_rows, left] = context
                dq[mine_rows, left] = jnp.dot(d_score, key, preferred_element_type=FONE).astype(HALF)
            for part in range(2):
                column = 2 + part - pair
                if 0 <= column < 3:
                    cut = slice(column * PAIR, (column + 1) * PAIR)
                    k_term = tn(d_score[:, cut], query)
                    v_term = tn(prob_b[:, cut], d_context)
                    first = d_key[part] is None
                    d_key[part] = k_term if first else d_key[part] + k_term
                    d_value[part] = v_term if first else d_value[part] + v_term
        for part in range(2):
            cut = slice(part * PAIR, (part + 1) * PAIR)
            dkv[cut, left] = d_key[part].astype(HALF)
            dkv[cut, right] = d_value[part].astype(HALF)

    for weight in range(4):
        await_copies(whole, weight, w_sems)
    for head in range(N_HEAD):
        terms[head, 0] = nt(ctx[...], piece(whole, 3, head)).astype(HALF)
        terms[head, 1] = nt(dq[...], piece(whole, 0, head)).astype(HALF)
        source_term = nt(dkv[:, :WIDTH], piece(whole, 1, head))
        source_term = source_term + nt(dkv[:, WIDTH:], piece(whole, 2, head))
        terms[head, 2] = source_term.astype(HALF)
        pltpu.make_async_copy(terms.at[head], out.at[head], o_sems.at[head]).start()
    for head in range(N_HEAD):
        pltpu.make_async_copy(terms.at[head], out.at[head], o_sems.at[head]).wait()


VMEM = pl.BlockSpec(memory_space=pltpu.VMEM)
ANY = pl.BlockSpec(memory_space=pl.ANY)


def shaped(*dims):
    return jax.ShapeDtypeStruct(dims, HALF)


def scratch(*dims):
    return pltpu.VMEM(dims, HALF)


def copies(count):
    return pltpu.SemaphoreType.DMA((count,))


MATRICES = scratch(4, N_SEQ, SHARD, WIDTH)


def call_project(acts, gathered, band):
    return pl.pallas_call(
        project,
        name="project",
        out_shape=(
            shaped(ROWS, 2 * WIDTH),
            shaped(ROWS, 2 * WIDTH),
            shaped(5 * BLOCK + 16, 2 * WIDTH),
            shaped(4 * BLOCK + 16, 2 * WIDTH),
        ),
        in_specs=[ANY, ANY, VMEM],
        out_specs=(VMEM,) * 4,
        scratch_shapes=[MATRICES, scratch(3, ROWS, N_HEAD * WIDTH), copies(4), copies(3)],
    )(acts, gathered, band)


def call_attend(kv, qd, prev, after, band, gathered):
    return pl.pallas_call(
        attend,
        name="attend",
        out_shape=shaped(N_HEAD, 3, ROWS, WIDTH),
        in_specs=[VMEM, VMEM, VMEM, VMEM, VMEM, ANY],
        out_specs=ANY,
        scratch_shapes=[
            scratch(12 * BLOCK, 2 * WIDTH),
            scratch(8 * BLOCK, 2 * WIDTH),
            scratch(ROWS, WIDTH),
            scratch(ROWS, WIDTH),
            scratch(ROWS, 2 * WIDTH),
            scratch(N_HEAD, 3, ROWS, WIDTH),
            MATRICES,
            copies(4),
            copies(N_HEAD),
        ],
    )(kv, qd, prev, after, band, gathered)


def band_rows(band_start, band_end, shard):
    blocks = ROWS // BLOCK
    before = shard * blocks + jnp.arange(blocks, dtype=jnp.int32) - 1
    spare = jnp.zeros((8,), jnp.int32)
    offsets = jnp.concatenate([band_start - before, band_end - before, spare]).astype(HALF)
    return jnp.broadcast_to(offsets[:, None], (16, 2 * WIDTH))


def per_device(target, source, w_query, w_key, w_value, w_out, band_start, band_end, cotangent):
    shard = lax.axis_index("seq")
    band = band_rows(band_start, band_end, shard)

    w_mine = jnp.stack([w_query, w_key, w_value, w_out])
    w_z = lax.all_gather(w_mine, "seq", axis=0, axis_index_groups=Z_GROUPS)
    target, source, cotangent, w_z = lax.optimization_barrier((target, source, cotangent, w_z))
    gathered = lax.all_gather(w_z, "seq", axis=0, axis_index_groups=YC_GROUPS)
    acts = jnp.stack([target, source, cotangent])
    acts = jnp.broadcast_to(acts[None], (N_HEAD,) + acts.shape)
    acts = lax.all_to_all(acts, "head", 0, 0)
    acts, gathered, band = lax.optimization_barrier((acts, gathered, band))

    kv, qd, to_next, to_prev = call_project(acts, gathered, band)
    prev = passed_along(to_next, "seq", 1)
    after = passed_along(to_prev, "seq", -1)
    terms = call_attend(kv, qd, prev, after, band, gathered)
    terms = lax.all_to_all(terms, "head", 0, 0)
    return tuple(jnp.sum(terms[:, i].astype(FONE), axis=0).astype(HALF) for i in range(3))


def solution(mesh):
    sharded = P("seq", "head")
    in_specs = (sharded,) * 6 + (P("seq"), P("seq"), sharded)
    return jax.shard_map(
        per_device, mesh=mesh, in_specs=in_specs, out_specs=(sharded,) * 3, check_vma=False
    )
```

```python
import jax
import jax.numpy as jnp
from jax import lax
from jax.experimental import pallas as pl
from jax.experimental.pallas import tpu as pltpu
from jax.sharding import PartitionSpec as P

HEAD_DIM = 128
BLOCK = 64
MAXW = 3
N_Z, N_Y, N_CORE = 4, 8, 2
N_SEQ = N_Z * N_Y * N_CORE
N_HEAD = 8
ROWS = 256
WIDTH = 256
SHARD = 32
PAIR = 2 * BLOCK
REACH = 3 * PAIR
HALF = jnp.bfloat16
FONE = jnp.float32


Z_GROUPS = [
    [z * N_Y * N_CORE + k for z in range(N_Z)] for k in range(N_Y * N_CORE)
]
YC_GROUPS = [[z * N_Y * N_CORE + k for k in range(N_Y * N_CORE)] for z in range(N_Z)]


def passed_along(shard, axis, by):
    pairs = [(i, i + by) for i in range(N_SEQ) if 0 <= i + by < N_SEQ]
    return lax.ppermute(shard, axis, pairs)


def nt(left, right):
    return lax.dot_general(left, right, (((1,), (1,)), ((), ())), preferred_element_type=FONE)


def tn(left, right):
    return lax.dot_general(left, right, (((0,), (0,)), ((), ())), preferred_element_type=FONE)


def fetch_weight(gathered, weight, whole, sems):
    per = N_SEQ // N_HEAD
    for head in range(N_HEAD):
        pltpu.make_async_copy(
            gathered.at[pl.ds(per * (head % 2), per), head // 2, weight],
            whole.at[weight, pl.ds(per * head, per)],
            sems.at[weight],
        ).start()


def band_rows(offsets):
    row = lax.broadcasted_iota(jnp.int32, (16, 2 * WIDTH), 0)
    rows = jnp.zeros((16, 2 * WIDTH), FONE)
    for i in range(8):
        rows = jnp.where(row == i, offsets[i].astype(FONE), rows)
    return rows


def await_copies(ref, slot, sems):
    pltpu.make_async_copy(ref.at[slot], ref.at[slot], sems.at[slot]).wait()


def piece(whole, weight, head):
    per = N_SEQ // N_HEAD
    return whole[weight, per * head : per * (head + 1)].reshape(WIDTH, WIDTH)


def project(offsets, acts, gathered, kv, qd, to_next, to_prev, whole, w_sems):
    for weight in (1, 2, 0, 3):
        fetch_weight(gathered, weight, whole, w_sems)
    band = band_rows(offsets).astype(HALF)

    def product(which, weight):
        left = jnp.concatenate([acts[head, which] for head in range(N_HEAD)], axis=1)
        await_copies(whole, weight, w_sems)
        right = whole[weight].reshape(N_SEQ * SHARD, WIDTH)
        return jnp.dot(left, right, preferred_element_type=FONE).astype(HALF)

    kv[:, :WIDTH] = product(1, 1)
    kv[:, WIDTH:] = product(1, 2)
    qd[:, :WIDTH] = product(0, 0)
    qd[:, WIDTH:] = product(2, 3)
    to_next[: 3 * BLOCK] = kv[BLOCK:]
    to_next[3 * BLOCK : 5 * BLOCK] = qd[2 * BLOCK :]
    to_next[5 * BLOCK :] = band
    to_prev[: 3 * BLOCK] = kv[: 3 * BLOCK]
    to_prev[3 * BLOCK : 4 * BLOCK] = qd[:BLOCK]
    to_prev[4 * BLOCK :] = band


def attend(offsets, kv, qd, prev, after, whole, terms, kvw, qdw, ctx, dq, dkv):
    kvw[:BLOCK] = jnp.zeros((BLOCK, 2 * WIDTH), HALF)
    kvw[BLOCK : 4 * BLOCK] = prev[: 3 * BLOCK]
    kvw[4 * BLOCK : 8 * BLOCK] = kv[...]
    kvw[8 * BLOCK : 11 * BLOCK] = after[: 3 * BLOCK]
    kvw[11 * BLOCK :] = jnp.zeros((BLOCK, 2 * WIDTH), HALF)
    qdw[: 2 * BLOCK] = prev[3 * BLOCK : 5 * BLOCK]
    qdw[2 * BLOCK : 6 * BLOCK] = qd[...]
    qdw[6 * BLOCK : 7 * BLOCK] = after[3 * BLOCK : 4 * BLOCK]
    qdw[7 * BLOCK :] = jnp.zeros((BLOCK, 2 * WIDTH), HALF)

    own = band_rows(offsets)[:, :REACH]
    back = prev[5 * BLOCK :].astype(FONE)[:, :REACH]
    ahead = after[4 * BLOCK :].astype(FONE)[:, :REACH]
    rows = [(back, 2), (back, 3), (own, 0), (own, 1), (own, 2), (own, 3), (ahead, 0), (own, 8)]
    lows = [source[i : i + 1] for source, i in rows]
    highs = [source[i + 4 : i + 5] for source, i in rows]
    lower = lax.broadcasted_iota(jnp.int32, (PAIR, REACH), 0) // BLOCK
    offset = lax.broadcasted_iota(jnp.int32, (PAIR, REACH), 1) // BLOCK - lower - 1
    offset = offset.astype(FONE)
    scale = HEAD_DIM**-0.5
    for head in range(2):
        left = slice(head * HEAD_DIM, (head + 1) * HEAD_DIM)
        right = slice(WIDTH + head * HEAD_DIM, WIDTH + (head + 1) * HEAD_DIM)
        d_key = [None, None]
        d_value = [None, None]
        for pair in range(4):
            low = jnp.where(lower == 0, lows[2 * pair], lows[2 * pair + 1])
            high = jnp.where(lower == 0, highs[2 * pair], highs[2 * pair + 1])
            visible = (offset >= low) & (offset < high)
            here = slice(pair * PAIR, (pair + 1) * PAIR)
            there = slice(pair * PAIR, pair * PAIR + REACH)
            query, d_context = qdw[here, left], qdw[here, right]
            key, value = kvw[there, left], kvw[there, right]
            score = jnp.where(visible, nt(query, key) * scale, -jnp.inf)
            top = jnp.max(score, axis=-1, keepdims=True)
            expo = jnp.where(visible, jnp.exp(score - top), 0.0)
            prob = expo / jnp.maximum(jnp.sum(expo, axis=-1, keepdims=True), 0.5)
            prob_b = prob.astype(HALF)
            context = jnp.dot(prob_b, value, preferred_element_type=FONE).astype(HALF)
            delta = jnp.sum(
                d_context.astype(FONE) * context.astype(FONE), axis=-1, keepdims=True
            )
            d_prob = nt(d_context, value)
            d_score = (prob * (d_prob - delta) * scale).astype(HALF)
            if pair in (1, 2):
                mine_rows = slice((pair - 1) * PAIR, pair * PAIR)
                ctx[mine_rows, left] = context
                dq[mine_rows, left] = jnp.dot(d_score, key, preferred_element_type=FONE).astype(HALF)
            for part in range(2):
                column = 2 + part - pair
                if 0 <= column < 3:
                    cut = slice(column * PAIR, (column + 1) * PAIR)
                    k_term = tn(d_score[:, cut], query)
                    v_term = tn(prob_b[:, cut], d_context)
                    first = d_key[part] is None
                    d_key[part] = k_term if first else d_key[part] + k_term
                    d_value[part] = v_term if first else d_value[part] + v_term
        for part in range(2):
            cut = slice(part * PAIR, (part + 1) * PAIR)
            dkv[cut, left] = d_key[part].astype(HALF)
            dkv[cut, right] = d_value[part].astype(HALF)

    for head in range(N_HEAD):
        terms[head, 0] = nt(ctx[...], piece(whole, 3, head)).astype(HALF)
        terms[head, 1] = nt(dq[...], piece(whole, 0, head)).astype(HALF)
        source_term = nt(dkv[:, :WIDTH], piece(whole, 1, head))
        source_term = source_term + nt(dkv[:, WIDTH:], piece(whole, 2, head))
        terms[head, 2] = source_term.astype(HALF)


SMEM = pl.BlockSpec(memory_space=pltpu.SMEM)
VMEM = pl.BlockSpec(memory_space=pltpu.VMEM)


def shaped(*dims):
    return pltpu.VMEM(dims, HALF)


def in_vmem(*arrays):
    return [pltpu.with_memory_space_constraint(array, pltpu.VMEM) for array in arrays]


def scratch(*dims):
    return pltpu.VMEM(dims, HALF)


def copies(count):
    return pltpu.SemaphoreType.DMA((count,))


MATRICES = scratch(4, N_SEQ, SHARD, WIDTH)
HBM = pl.BlockSpec(memory_space=pltpu.HBM)
ROOM = pltpu.CompilerParams(vmem_limit_bytes=28 << 20)


def call_project(offsets, acts, gathered):
    return pl.pallas_call(
        project,
        name="project",
        out_shape=(
            shaped(ROWS, 2 * WIDTH),
            shaped(ROWS, 2 * WIDTH),
            shaped(5 * BLOCK + 16, 2 * WIDTH),
            shaped(4 * BLOCK + 16, 2 * WIDTH),
            MATRICES,
        ),
        in_specs=[SMEM, VMEM, HBM],
        out_specs=(VMEM,) * 5,
        scratch_shapes=[copies(4)],
        compiler_params=ROOM,
    )(offsets, *in_vmem(acts), pltpu.with_memory_space_constraint(gathered, pltpu.HBM))


def call_attend(offsets, kv, qd, prev, after, whole):
    return pl.pallas_call(
        attend,
        name="attend",
        out_shape=shaped(N_HEAD, 3, ROWS, WIDTH),
        in_specs=[SMEM] + [VMEM] * 5,
        out_specs=VMEM,
        scratch_shapes=[
            scratch(12 * BLOCK, 2 * WIDTH),
            scratch(8 * BLOCK, 2 * WIDTH),
            scratch(ROWS, WIDTH),
            scratch(ROWS, WIDTH),
            scratch(ROWS, 2 * WIDTH),
        ],
        compiler_params=ROOM,
    )(offsets, *in_vmem(kv, qd, prev, after, whole))


def band_offsets(band_start, band_end, shard):
    blocks = ROWS // BLOCK
    before = shard * blocks + jnp.arange(blocks, dtype=jnp.int32) - 1
    return jnp.concatenate([band_start - before, band_end - before])


def per_device(target, source, w_query, w_key, w_value, w_out, band_start, band_end, cotangent):
    shard = lax.axis_index("seq")
    offsets = band_offsets(band_start, band_end, shard)

    w_mine = jnp.stack([w_query, w_key, w_value, w_out])
    w_z = lax.all_gather(w_mine, "seq", axis=0, axis_index_groups=Z_GROUPS)
    target, source, cotangent, w_z = lax.optimization_barrier((target, source, cotangent, w_z))
    gathered = lax.all_gather(w_z, "seq", axis=0, axis_index_groups=YC_GROUPS)
    acts = jnp.stack([target, source, cotangent])
    acts = jnp.broadcast_to(acts[None], (N_HEAD,) + acts.shape)
    acts = lax.all_to_all(acts, "head", 0, 0)
    acts, gathered, offsets = lax.optimization_barrier((acts, gathered, offsets))

    kv, qd, to_next, to_prev, whole = call_project(offsets, acts, gathered)
    prev = passed_along(to_next, "seq", 1)
    after = passed_along(to_prev, "seq", -1)
    terms = call_attend(offsets, kv, qd, prev, after, whole)
    terms = lax.all_to_all(terms, "head", 0, 0)
    return tuple(jnp.sum(terms[:, i].astype(FONE), axis=0).astype(HALF) for i in range(3))


def solution(mesh):
    sharded = P("seq", "head")
    in_specs = (sharded,) * 6 + (P("seq"), P("seq"), sharded)
    return jax.shard_map(
        per_device, mesh=mesh, in_specs=in_specs, out_specs=(sharded,) * 3, check_vma=False
    )
```

```python
import jax
import jax.numpy as jnp
from jax import lax
from jax.experimental import pallas as pl
from jax.experimental.pallas import tpu as pltpu
from jax.sharding import PartitionSpec as P

HEAD_DIM = 128
BLOCK = 64
MAXW = 3
N_Z, N_Y, N_CORE = 4, 8, 2
N_SEQ = N_Z * N_Y * N_CORE
N_HEAD = 8
ROWS = 256
WIDTH = 256
SHARD = 32
PAIR = 2 * BLOCK
REACH = 3 * PAIR
HALF = jnp.bfloat16
FONE = jnp.float32


Z_GROUPS = [
    [z * N_Y * N_CORE + k for z in range(N_Z)] for k in range(N_Y * N_CORE)
]
YC_GROUPS = [[z * N_Y * N_CORE + k for k in range(N_Y * N_CORE)] for z in range(N_Z)]


def passed_along(shard, axis, by):
    pairs = [(i, i + by) for i in range(N_SEQ) if 0 <= i + by < N_SEQ]
    return lax.ppermute(shard, axis, pairs)


def nt(left, right):
    return lax.dot_general(left, right, (((1,), (1,)), ((), ())), preferred_element_type=FONE)


def tn(left, right):
    return lax.dot_general(left, right, (((0,), (0,)), ((), ())), preferred_element_type=FONE)


def fetch_weight(gathered, weight, whole, sems):
    per = N_Y * N_CORE
    for z in range(N_Z):
        pltpu.make_async_copy(
            gathered.at[:, z, weight], whole.at[weight, pl.ds(per * z, per)], sems.at[weight]
        ).start()


def band_rows(offsets):
    row = lax.broadcasted_iota(jnp.int32, (16, 2 * WIDTH), 0)
    rows = jnp.zeros((16, 2 * WIDTH), FONE)
    for i in range(8):
        rows = jnp.where(row == i, offsets[i].astype(FONE), rows)
    return rows


def await_copies(ref, slot, sems):
    pltpu.make_async_copy(ref.at[slot], ref.at[slot], sems.at[slot]).wait()


def piece(whole, weight, head):
    per = N_SEQ // N_HEAD
    return whole[weight, per * head : per * (head + 1)].reshape(WIDTH, WIDTH)


def project(offsets, acts, gathered, kv, qd, to_next, to_prev, whole, w_sems):
    for weight in (1, 2, 0, 3):
        fetch_weight(gathered, weight, whole, w_sems)
    band = band_rows(offsets).astype(HALF)

    def product(which, weight):
        await_copies(whole, weight, w_sems)
        parts = [
            jnp.dot(acts[head, which], piece(whole, weight, head), preferred_element_type=FONE)
            for head in range(N_HEAD)
        ]
        while len(parts) > 1:
            parts = [parts[i] + parts[i + 1] for i in range(0, len(parts), 2)]
        return parts[0].astype(HALF)

    kv[:, :WIDTH] = product(1, 1)
    kv[:, WIDTH:] = product(1, 2)
    qd[:, :WIDTH] = product(0, 0)
    qd[:, WIDTH:] = product(2, 3)
    to_next[: 3 * BLOCK] = kv[BLOCK:]
    to_next[3 * BLOCK : 5 * BLOCK] = qd[2 * BLOCK :]
    to_next[5 * BLOCK :] = band
    to_prev[: 3 * BLOCK] = kv[: 3 * BLOCK]
    to_prev[3 * BLOCK : 4 * BLOCK] = qd[:BLOCK]
    to_prev[4 * BLOCK :] = band


def attend(offsets, kv, qd, prev, after, whole, terms, kvw, qdw, ctx, dq, dkv, bias):
    kvw[:BLOCK] = jnp.zeros((BLOCK, 2 * WIDTH), HALF)
    kvw[BLOCK : 4 * BLOCK] = prev[: 3 * BLOCK]
    kvw[4 * BLOCK : 8 * BLOCK] = kv[...]
    kvw[8 * BLOCK : 11 * BLOCK] = after[: 3 * BLOCK]
    kvw[11 * BLOCK :] = jnp.zeros((BLOCK, 2 * WIDTH), HALF)
    qdw[: 2 * BLOCK] = prev[3 * BLOCK : 5 * BLOCK]
    qdw[2 * BLOCK : 6 * BLOCK] = qd[...]
    qdw[6 * BLOCK : 7 * BLOCK] = after[3 * BLOCK : 4 * BLOCK]
    qdw[7 * BLOCK :] = jnp.zeros((BLOCK, 2 * WIDTH), HALF)

    own = band_rows(offsets)[:, :REACH]
    back = prev[5 * BLOCK :].astype(FONE)[:, :REACH]
    ahead = after[4 * BLOCK :].astype(FONE)[:, :REACH]
    rows = [(back, 2), (back, 3), (own, 0), (own, 1), (own, 2), (own, 3), (ahead, 0), (own, 8)]
    lows = [source[i : i + 1] for source, i in rows]
    highs = [source[i + 4 : i + 5] for source, i in rows]
    lower = lax.broadcasted_iota(jnp.int32, (PAIR, REACH), 0) // BLOCK
    offset = lax.broadcasted_iota(jnp.int32, (PAIR, REACH), 1) // BLOCK - lower - 1
    offset = offset.astype(FONE)
    scale = HEAD_DIM**-0.5
    for pair in range(4):
        low = jnp.where(lower == 0, lows[2 * pair], lows[2 * pair + 1])
        high = jnp.where(lower == 0, highs[2 * pair], highs[2 * pair + 1])
        bias[pair] = jnp.where((offset >= low) & (offset < high), 0.0, -1e30)
    for head in range(2):
        left = slice(head * HEAD_DIM, (head + 1) * HEAD_DIM)
        right = slice(WIDTH + head * HEAD_DIM, WIDTH + (head + 1) * HEAD_DIM)
        d_key = [None, None]
        d_value = [None, None]
        for pair in range(4):
            count = BLOCK if pair == 3 else PAIR
            here = slice(pair * PAIR, pair * PAIR + count)
            there = slice(pair * PAIR, pair * PAIR + REACH)
            query, d_context = qdw[here, left], qdw[here, right]
            key, value = kvw[there, left], kvw[there, right]
            score = nt(query, key) * scale + bias[pair, :count]
            expo = jnp.exp(score - jnp.max(score, axis=-1, keepdims=True))
            prob = expo * (1.0 / jnp.sum(expo, axis=-1, keepdims=True))
            prob_b = prob.astype(HALF)
            context = jnp.dot(prob_b, value, preferred_element_type=FONE).astype(HALF)
            delta = jnp.sum(
                d_context.astype(FONE) * context.astype(FONE), axis=-1, keepdims=True
            )
            own_pair = pair in (1, 2)
            used = slice(0, REACH) if own_pair else slice(2 * PAIR, REACH) if pair == 0 else slice(0, PAIR)
            d_prob = nt(d_context, value[used])
            d_score = (prob[:, used] * (d_prob - delta) * scale).astype(HALF)
            if own_pair:
                mine_rows = slice((pair - 1) * PAIR, pair * PAIR)
                ctx[mine_rows, left] = context
                dq[mine_rows, left] = jnp.dot(d_score, key, preferred_element_type=FONE).astype(HALF)
            for part in range(2):
                column = 2 + part - pair
                if 0 <= column < 3:
                    cut = slice(column * PAIR, (column + 1) * PAIR)
                    shifted = slice(cut.start - used.start, cut.stop - used.start)
                    k_term = tn(d_score[:, shifted], query)
                    v_term = tn(prob_b[:, cut], d_context)
                    first = d_key[part] is None
                    d_key[part] = k_term if first else d_key[part] + k_term
                    d_value[part] = v_term if first else d_value[part] + v_term
        for part in range(2):
            cut = slice(part * PAIR, (part + 1) * PAIR)
            dkv[cut, left] = d_key[part].astype(HALF)
            dkv[cut, right] = d_value[part].astype(HALF)

    for head in range(N_HEAD):
        terms[head, 0] = nt(ctx[...], piece(whole, 3, head)).astype(HALF)
        terms[head, 1] = nt(dq[...], piece(whole, 0, head)).astype(HALF)
        source_term = nt(dkv[:, :WIDTH], piece(whole, 1, head))
        source_term = source_term + nt(dkv[:, WIDTH:], piece(whole, 2, head))
        terms[head, 2] = source_term.astype(HALF)


SMEM = pl.BlockSpec(memory_space=pltpu.SMEM)
VMEM = pl.BlockSpec(memory_space=pltpu.VMEM)


def shaped(*dims):
    return pltpu.VMEM(dims, HALF)


def in_vmem(*arrays):
    return [pltpu.with_memory_space_constraint(array, pltpu.VMEM) for array in arrays]


def scratch(*dims):
    return pltpu.VMEM(dims, HALF)


def copies(count):
    return pltpu.SemaphoreType.DMA((count,))


MATRICES = scratch(4, N_SEQ, SHARD, WIDTH)
HBM = pl.BlockSpec(memory_space=pltpu.HBM)
ROOM = pltpu.CompilerParams(vmem_limit_bytes=28 << 20)


def call_project(offsets, acts, gathered):
    return pl.pallas_call(
        project,
        name="project",
        out_shape=(
            shaped(ROWS, 2 * WIDTH),
            shaped(ROWS, 2 * WIDTH),
            shaped(5 * BLOCK + 16, 2 * WIDTH),
            shaped(4 * BLOCK + 16, 2 * WIDTH),
            MATRICES,
        ),
        in_specs=[SMEM, VMEM, HBM],
        out_specs=(VMEM,) * 5,
        scratch_shapes=[copies(4)],
        compiler_params=ROOM,
    )(offsets, *in_vmem(acts), pltpu.with_memory_space_constraint(gathered, pltpu.HBM))


def call_attend(offsets, kv, qd, prev, after, whole):
    return pl.pallas_call(
        attend,
        name="attend",
        out_shape=shaped(N_HEAD, 3, ROWS, WIDTH),
        in_specs=[SMEM] + [VMEM] * 5,
        out_specs=VMEM,
        scratch_shapes=[
            scratch(12 * BLOCK, 2 * WIDTH),
            scratch(8 * BLOCK, 2 * WIDTH),
            scratch(ROWS, WIDTH),
            scratch(ROWS, WIDTH),
            scratch(ROWS, 2 * WIDTH),
            pltpu.VMEM((4, PAIR, REACH), FONE),
        ],
        compiler_params=ROOM,
    )(offsets, *in_vmem(kv, qd, prev, after, whole))


def band_offsets(band_start, band_end, shard):
    blocks = ROWS // BLOCK
    before = shard * blocks + jnp.arange(blocks, dtype=jnp.int32) - 1
    return jnp.concatenate([band_start - before, band_end - before])


def per_device(target, source, w_query, w_key, w_value, w_out, band_start, band_end, cotangent):
    shard = lax.axis_index("seq")
    offsets = band_offsets(band_start, band_end, shard)

    w_mine = jnp.stack([w_query, w_key, w_value, w_out])
    w_z = lax.all_gather(w_mine, "seq", axis=0, axis_index_groups=Z_GROUPS)
    target, source, cotangent, w_z = lax.optimization_barrier((target, source, cotangent, w_z))
    gathered = lax.all_gather(w_z, "seq", axis=0, axis_index_groups=YC_GROUPS)
    acts = jnp.stack([target, source, cotangent])
    acts = jnp.broadcast_to(acts[None], (N_HEAD,) + acts.shape)
    acts = lax.all_to_all(acts, "head", 0, 0)
    acts, gathered, offsets = lax.optimization_barrier((acts, gathered, offsets))

    kv, qd, to_next, to_prev, whole = call_project(offsets, acts, gathered)
    prev = passed_along(to_next, "seq", 1)
    after = passed_along(to_prev, "seq", -1)
    terms = call_attend(offsets, kv, qd, prev, after, whole)
    terms = lax.all_to_all(terms, "head", 0, 0)
    return tuple(jnp.sum(terms[:, i].astype(FONE), axis=0).astype(HALF) for i in range(3))


def solution(mesh):
    sharded = P("seq", "head")
    in_specs = (sharded,) * 6 + (P("seq"), P("seq"), sharded)
    return jax.shard_map(
        per_device, mesh=mesh, in_specs=in_specs, out_specs=(sharded,) * 3, check_vma=False
    )
```

```python
import jax
import jax.numpy as jnp
from jax import lax
from jax.experimental import pallas as pl
from jax.experimental.pallas import tpu as pltpu
from jax.sharding import PartitionSpec as P

HEAD_DIM = 128
BLOCK = 64
MAXW = 3
N_Z, N_Y, N_CORE = 4, 8, 2
N_SEQ = N_Z * N_Y * N_CORE
N_HEAD = 8
ROWS = 256
WIDTH = 256
SHARD = 32
PAIR = 2 * BLOCK
REACH = 3 * PAIR
HALF = jnp.bfloat16
FONE = jnp.float32


Z_GROUPS = [
    [z * N_Y * N_CORE + k for z in range(N_Z)] for k in range(N_Y * N_CORE)
]
YC_GROUPS = [[z * N_Y * N_CORE + k for k in range(N_Y * N_CORE)] for z in range(N_Z)]


def passed_along(shard, axis, by):
    pairs = [(i, i + by) for i in range(N_SEQ) if 0 <= i + by < N_SEQ]
    return lax.ppermute(shard, axis, pairs)


def nt(left, right):
    return lax.dot_general(left, right, (((1,), (1,)), ((), ())), preferred_element_type=FONE)


def tn(left, right):
    return lax.dot_general(left, right, (((0,), (0,)), ((), ())), preferred_element_type=FONE)


def fetch_weight(gathered, weight, whole, sems):
    per = N_Y * N_CORE
    for z in range(N_Z):
        pltpu.make_async_copy(
            gathered.at[:, z, weight], whole.at[weight, pl.ds(per * z, per)], sems.at[weight]
        ).start()


def band_rows(offsets):
    row = lax.broadcasted_iota(jnp.int32, (16, 2 * WIDTH), 0)
    rows = jnp.zeros((16, 2 * WIDTH), FONE)
    for i in range(8):
        rows = jnp.where(row == i, offsets[i].astype(FONE), rows)
    return rows


def await_copies(ref, slot, sems):
    pltpu.make_async_copy(ref.at[slot], ref.at[slot], sems.at[slot]).wait()


def piece(whole, weight, head):
    per = N_SEQ // N_HEAD
    return whole[weight, per * head : per * (head + 1)].reshape(WIDTH, WIDTH)


def project(offsets, acts, gathered, kv, qd, to_next, to_prev, whole, w_sems):
    for weight in (1, 2, 0, 3):
        fetch_weight(gathered, weight, whole, w_sems)
    band = band_rows(offsets).astype(HALF)

    def product(which, weight):
        await_copies(whole, weight, w_sems)
        parts = [
            jnp.dot(acts[head, which], piece(whole, weight, head), preferred_element_type=FONE)
            for head in range(N_HEAD)
        ]
        while len(parts) > 1:
            parts = [parts[i] + parts[i + 1] for i in range(0, len(parts), 2)]
        return parts[0].astype(HALF)

    kv[:, :WIDTH] = product(1, 1)
    kv[:, WIDTH:] = product(1, 2)
    qd[:, :WIDTH] = product(0, 0)
    qd[:, WIDTH:] = product(2, 3)
    to_next[:PAIR] = kv[PAIR:]
    to_next[PAIR : 2 * PAIR] = qd[PAIR:]
    to_next[2 * PAIR :] = band
    to_prev[:PAIR] = kv[:PAIR]
    to_prev[PAIR : PAIR + BLOCK] = qd[:BLOCK]
    to_prev[PAIR + BLOCK :] = band


def attend(offsets, kv, qd, prev, after, whole, terms, kvw, qdw, ctx, dq, dkv, bias):
    kvw[:PAIR] = prev[:PAIR]
    kvw[PAIR : 3 * PAIR] = kv[...]
    kvw[3 * PAIR :] = after[:PAIR]
    qdw[:PAIR] = prev[PAIR : 2 * PAIR]
    qdw[PAIR : 3 * PAIR] = qd[...]
    qdw[3 * PAIR :] = after[PAIR : PAIR + BLOCK]

    own = band_rows(offsets)[:, :REACH]
    back = prev[2 * PAIR :].astype(FONE)[:, :REACH]
    ahead = after[PAIR + BLOCK :].astype(FONE)[:, :REACH]
    rows = [(back, 2), (back, 3), (own, 0), (own, 1), (own, 2), (own, 3), (ahead, 0), (ahead, 0)]
    lows = [source[i : i + 1] for source, i in rows]
    highs = [source[i + 4 : i + 5] for source, i in rows]
    lower = lax.broadcasted_iota(jnp.int32, (PAIR, REACH), 0) // BLOCK
    column = lax.broadcasted_iota(jnp.int32, (PAIR, REACH), 1) // BLOCK
    scale = HEAD_DIM**-0.5
    windows = ((0, 2 * PAIR), (0, REACH), (PAIR, REACH), (2 * PAIR, 2 * PAIR))
    for pair in range(4):
        offset = (column - lower + (1 if pair == 0 else -1)).astype(FONE)
        low = jnp.where(lower == 0, lows[2 * pair], lows[2 * pair + 1])
        high = jnp.where(lower == 0, highs[2 * pair], highs[2 * pair + 1])
        bias[pair] = jnp.where((offset >= low) & (offset < high), 0.0, -1e30)
    for head in range(2):
        left = slice(head * HEAD_DIM, (head + 1) * HEAD_DIM)
        right = slice(WIDTH + head * HEAD_DIM, WIDTH + (head + 1) * HEAD_DIM)
        d_key = [None, None]
        d_value = [None, None]
        for pair, (start, span) in enumerate(windows):
            own_pair = pair in (1, 2)
            count = BLOCK if pair == 3 else PAIR
            here = slice(pair * PAIR, pair * PAIR + count)
            there = slice(start, start + span)
            query, d_context = qdw[here, left], qdw[here, right]
            key, value = kvw[there, left], kvw[there, right]
            mask = bias[pair, :count, :span]
            score = nt(query, key) * scale + mask
            expo = jnp.exp(score - jnp.max(score, axis=-1, keepdims=True))
            total = jnp.sum(expo, axis=-1, keepdims=True)
            if not own_pair:
                expo = jnp.where(mask < 0.0, 0.0, expo)
            prob = expo * (1.0 / total)
            prob_b = prob.astype(HALF)
            context = jnp.dot(prob_b, value, preferred_element_type=FONE).astype(HALF)
            delta = jnp.sum(
                d_context.astype(FONE) * context.astype(FONE), axis=-1, keepdims=True
            )
            parts = [part for part in range(2) if start <= (1 + part) * PAIR < start + span]
            used = slice(0, span)
            if not own_pair:
                used = slice(PAIR * (1 + parts[0]) - start, PAIR * (2 + parts[0]) - start)
            d_prob = nt(d_context, value[used])
            d_score = (prob[:, used] * (d_prob - delta) * scale).astype(HALF)
            if own_pair:
                mine_rows = slice((pair - 1) * PAIR, pair * PAIR)
                ctx[mine_rows, left] = context
                dq[mine_rows, left] = jnp.dot(d_score, key, preferred_element_type=FONE).astype(HALF)
            for part in parts if own_pair else parts[:1]:
                at = (1 + part) * PAIR - start
                k_term = tn(d_score[:, at - used.start : at - used.start + PAIR], query)
                v_term = tn(prob_b[:, at : at + PAIR], d_context)
                first = d_key[part] is None
                d_key[part] = k_term if first else d_key[part] + k_term
                d_value[part] = v_term if first else d_value[part] + v_term
        for part in range(2):
            cut = slice(part * PAIR, (part + 1) * PAIR)
            dkv[cut, left] = d_key[part].astype(HALF)
            dkv[cut, right] = d_value[part].astype(HALF)

    for head in range(N_HEAD):
        terms[head, 0] = nt(ctx[...], piece(whole, 3, head)).astype(HALF)
        terms[head, 1] = nt(dq[...], piece(whole, 0, head)).astype(HALF)
        source_term = nt(dkv[:, :WIDTH], piece(whole, 1, head))
        source_term = source_term + nt(dkv[:, WIDTH:], piece(whole, 2, head))
        terms[head, 2] = source_term.astype(HALF)


SMEM = pl.BlockSpec(memory_space=pltpu.SMEM)
VMEM = pl.BlockSpec(memory_space=pltpu.VMEM)


def shaped(*dims):
    return pltpu.VMEM(dims, HALF)


def in_vmem(*arrays):
    return [pltpu.with_memory_space_constraint(array, pltpu.VMEM) for array in arrays]


def scratch(*dims):
    return pltpu.VMEM(dims, HALF)


def copies(count):
    return pltpu.SemaphoreType.DMA((count,))


MATRICES = scratch(4, N_SEQ, SHARD, WIDTH)
HBM = pl.BlockSpec(memory_space=pltpu.HBM)
ROOM = pltpu.CompilerParams(vmem_limit_bytes=28 << 20)


def call_project(offsets, acts, gathered):
    return pl.pallas_call(
        project,
        name="project",
        out_shape=(
            shaped(ROWS, 2 * WIDTH),
            shaped(ROWS, 2 * WIDTH),
            shaped(2 * PAIR + 16, 2 * WIDTH),
            shaped(PAIR + BLOCK + 16, 2 * WIDTH),
            MATRICES,
        ),
        in_specs=[SMEM, VMEM, HBM],
        out_specs=(VMEM,) * 5,
        scratch_shapes=[copies(4)],
        compiler_params=ROOM,
    )(offsets, *in_vmem(acts), pltpu.with_memory_space_constraint(gathered, pltpu.HBM))


def call_attend(offsets, kv, qd, prev, after, whole):
    return pl.pallas_call(
        attend,
        name="attend",
        out_shape=shaped(N_HEAD, 3, ROWS, WIDTH),
        in_specs=[SMEM] + [VMEM] * 5,
        out_specs=VMEM,
        scratch_shapes=[
            scratch(4 * PAIR, 2 * WIDTH),
            scratch(3 * PAIR + BLOCK, 2 * WIDTH),
            scratch(ROWS, WIDTH),
            scratch(ROWS, WIDTH),
            scratch(ROWS, 2 * WIDTH),
            pltpu.VMEM((4, PAIR, REACH), FONE),
        ],
        compiler_params=ROOM,
    )(offsets, *in_vmem(kv, qd, prev, after, whole))


def band_offsets(band_start, band_end, shard):
    blocks = ROWS // BLOCK
    before = shard * blocks + jnp.arange(blocks, dtype=jnp.int32) - 1
    return jnp.concatenate([band_start - before, band_end - before])


def per_device(target, source, w_query, w_key, w_value, w_out, band_start, band_end, cotangent):
    shard = lax.axis_index("seq")
    offsets = band_offsets(band_start, band_end, shard)

    w_mine = jnp.stack([w_query, w_key, w_value, w_out])
    w_z = lax.all_gather(w_mine, "seq", axis=0, axis_index_groups=Z_GROUPS)
    target, source, cotangent, w_z = lax.optimization_barrier((target, source, cotangent, w_z))
    gathered = lax.all_gather(w_z, "seq", axis=0, axis_index_groups=YC_GROUPS)
    acts = jnp.stack([target, source, cotangent])
    acts = jnp.broadcast_to(acts[None], (N_HEAD,) + acts.shape)
    acts = lax.all_to_all(acts, "head", 0, 0)
    acts, gathered, offsets = lax.optimization_barrier((acts, gathered, offsets))

    kv, qd, to_next, to_prev, whole = call_project(offsets, acts, gathered)
    prev = passed_along(to_next, "seq", 1)
    after = passed_along(to_prev, "seq", -1)
    terms = call_attend(offsets, kv, qd, prev, after, whole)
    terms = lax.all_to_all(terms, "head", 0, 0)
    return tuple(jnp.sum(terms[:, i].astype(FONE), axis=0).astype(HALF) for i in range(3))


def solution(mesh):
    sharded = P("seq", "head")
    in_specs = (sharded,) * 6 + (P("seq"), P("seq"), sharded)
    return jax.shard_map(
        per_device, mesh=mesh, in_specs=in_specs, out_specs=(sharded,) * 3, check_vma=False
    )
```

```python
import jax
import jax.numpy as jnp
from jax import lax
from jax.experimental import pallas as pl
from jax.experimental.pallas import tpu as pltpu
from jax.sharding import PartitionSpec as P

HEAD_DIM = 128
BLOCK = 64
MAXW = 3
N_Z, N_Y, N_CORE = 4, 8, 2
N_SEQ = N_Z * N_Y * N_CORE
N_HEAD = 8
ROWS = 256
WIDTH = 256
SHARD = 32
PAIR = 2 * BLOCK
REACH = 3 * PAIR
HALF = jnp.bfloat16
FONE = jnp.float32


Z_GROUPS = [
    [z * N_Y * N_CORE + k for z in range(N_Z)] for k in range(N_Y * N_CORE)
]
YC_GROUPS = [[z * N_Y * N_CORE + k for k in range(N_Y * N_CORE)] for z in range(N_Z)]


def passed_along(shard, axis, by):
    pairs = [(i, i + by) for i in range(N_SEQ) if 0 <= i + by < N_SEQ]
    return lax.ppermute(shard, axis, pairs)


def nt(left, right):
    return lax.dot_general(left, right, (((1,), (1,)), ((), ())), preferred_element_type=FONE)


def tn(left, right):
    return lax.dot_general(left, right, (((0,), (0,)), ((), ())), preferred_element_type=FONE)


def fetch_weight(gathered, weight, whole, sems):
    per = N_Y * N_CORE
    for z in range(N_Z):
        pltpu.make_async_copy(
            gathered.at[:, z, weight], whole.at[weight, pl.ds(per * z, per)], sems.at[weight]
        ).start()


def band_rows(offsets):
    row = lax.broadcasted_iota(jnp.int32, (16, 2 * WIDTH), 0)
    rows = jnp.zeros((16, 2 * WIDTH), FONE)
    for i in range(8):
        rows = jnp.where(row == i, offsets[i].astype(FONE), rows)
    return rows


def await_copies(ref, slot, sems):
    pltpu.make_async_copy(ref.at[slot], ref.at[slot], sems.at[slot]).wait()


def piece(whole, weight, head):
    per = N_SEQ // N_HEAD
    return whole[weight, per * head : per * (head + 1)].reshape(WIDTH, WIDTH)


def project(offsets, acts, gathered, kv, qd, to_next, to_prev, whole, w_sems):
    for weight in (1, 2, 0, 3):
        fetch_weight(gathered, weight, whole, w_sems)
    band = band_rows(offsets).astype(HALF)

    def product(which, weight):
        await_copies(whole, weight, w_sems)
        parts = [
            jnp.dot(acts[head, which], piece(whole, weight, head), preferred_element_type=FONE)
            for head in range(N_HEAD)
        ]
        while len(parts) > 1:
            parts = [parts[i] + parts[i + 1] for i in range(0, len(parts), 2)]
        return parts[0].astype(HALF)

    kv[:, :WIDTH] = product(1, 1)
    kv[:, WIDTH:] = product(1, 2)
    qd[:, :WIDTH] = product(0, 0)
    qd[:, WIDTH:] = product(2, 3)
    to_next[:PAIR] = kv[PAIR:]
    to_next[PAIR : 2 * PAIR] = qd[PAIR:]
    to_next[2 * PAIR :] = band
    to_prev[:PAIR] = kv[:PAIR]
    to_prev[PAIR : PAIR + BLOCK] = qd[:BLOCK]
    to_prev[PAIR + BLOCK :] = band


def attend(offsets, kv, qd, prev, after, whole, terms, kvw, qdw, ctx, dq, grad, bias):
    kvw[:PAIR] = prev[:PAIR]
    kvw[PAIR : 3 * PAIR] = kv[...]
    kvw[3 * PAIR :] = after[:PAIR]
    qdw[:PAIR] = prev[PAIR : 2 * PAIR]
    qdw[PAIR : 3 * PAIR] = qd[...]
    qdw[3 * PAIR :] = after[PAIR : PAIR + BLOCK]

    own = band_rows(offsets)[:, :REACH]
    back = prev[2 * PAIR :].astype(FONE)[:, :REACH]
    ahead = after[PAIR + BLOCK :].astype(FONE)[:, :REACH]
    rows = [(back, 2), (back, 3), (own, 0), (own, 1), (own, 2), (own, 3), (ahead, 0), (ahead, 0)]
    lows = [source[i : i + 1] for source, i in rows]
    highs = [source[i + 4 : i + 5] for source, i in rows]
    lower = lax.broadcasted_iota(jnp.int32, (PAIR, REACH), 0) // BLOCK
    column = lax.broadcasted_iota(jnp.int32, (PAIR, REACH), 1) // BLOCK
    scale = HEAD_DIM**-0.5
    windows = ((0, 2 * PAIR), (0, REACH), (PAIR, REACH), (2 * PAIR, 2 * PAIR))
    for pair in range(4):
        offset = (column - lower + (1 if pair == 0 else -1)).astype(FONE)
        low = jnp.where(lower == 0, lows[2 * pair], lows[2 * pair + 1])
        high = jnp.where(lower == 0, highs[2 * pair], highs[2 * pair + 1])
        bias[pair] = jnp.where((offset >= low) & (offset < high), 0.0, -1e30)

    heads = [
        (slice(low, low + HEAD_DIM), slice(WIDTH + low, WIDTH + low + HEAD_DIM))
        for low in (0, HEAD_DIM)
    ]
    d_key = [[None, None], [None, None]]
    d_value = [[None, None], [None, None]]
    for pair, (start, span) in enumerate(windows):
        own_pair = pair in (1, 2)
        count = BLOCK if pair == 3 else PAIR
        here = slice(pair * PAIR, pair * PAIR + count)
        there = slice(start, start + span)
        parts = [part for part in range(2) if start <= (1 + part) * PAIR < start + span]
        used = slice(0, span)
        if not own_pair:
            parts = parts[:1]
            used = slice(PAIR * (1 + parts[0]) - start, PAIR * (2 + parts[0]) - start)
        scores = [nt(qdw[here, left], kvw[there, left]) for left, _ in heads]
        d_probs = [nt(qdw[here, right], kvw[there, right][used]) for _, right in heads]
        probs = []
        for score in scores:
            mask = bias[pair, :count, :span]
            score = score * scale + mask
            expo = jnp.exp(score - jnp.max(score, axis=-1, keepdims=True))
            total = jnp.sum(expo, axis=-1, keepdims=True)
            if not own_pair:
                expo = jnp.where(mask < 0.0, 0.0, expo)
            probs.append(expo * (1.0 / total))
        probs_b = [prob.astype(HALF) for prob in probs]
        contexts = [
            jnp.dot(prob_b, kvw[there, right], preferred_element_type=FONE).astype(HALF)
            for prob_b, (_, right) in zip(probs_b, heads)
        ]
        for head, (left, right) in enumerate(heads):
            query, d_context = qdw[here, left], qdw[here, right]
            for part in parts:
                at = (1 + part) * PAIR - start
                v_term = tn(probs_b[head][:, at : at + PAIR], d_context)
                last = d_value[head][part]
                d_value[head][part] = v_term if last is None else last + v_term
            delta = jnp.sum(
                d_context.astype(FONE) * contexts[head].astype(FONE), axis=-1, keepdims=True
            )
            d_score = (probs[head][:, used] * (d_probs[head] - delta) * scale).astype(HALF)
            if own_pair:
                mine_rows = slice((pair - 1) * PAIR, pair * PAIR)
                ctx[mine_rows, left] = contexts[head]
                dq[mine_rows, left] = jnp.dot(
                    d_score, kvw[there, left], preferred_element_type=FONE
                ).astype(HALF)
            for part in parts:
                at = (1 + part) * PAIR - start - used.start
                k_term = tn(d_score[:, at : at + PAIR], query)
                last = d_key[head][part]
                d_key[head][part] = k_term if last is None else last + k_term
    for head, (left, right) in enumerate(heads):
        for part in range(2):
            cut = slice(part * PAIR, (part + 1) * PAIR)
            grad[cut, left] = d_key[head][part].astype(HALF)
            grad[cut, right] = d_value[head][part].astype(HALF)
    for dest in range(N_HEAD):
        terms[dest, 0] = nt(ctx[...], piece(whole, 3, dest)).astype(HALF)
        terms[dest, 1] = nt(dq[...], piece(whole, 0, dest)).astype(HALF)
        source_term = nt(grad[:, :WIDTH], piece(whole, 1, dest))
        source_term = source_term + nt(grad[:, WIDTH:], piece(whole, 2, dest))
        terms[dest, 2] = source_term.astype(HALF)


SMEM = pl.BlockSpec(memory_space=pltpu.SMEM)
VMEM = pl.BlockSpec(memory_space=pltpu.VMEM)


def shaped(*dims):
    return pltpu.VMEM(dims, HALF)


def in_vmem(*arrays):
    return [pltpu.with_memory_space_constraint(array, pltpu.VMEM) for array in arrays]


def scratch(*dims):
    return pltpu.VMEM(dims, HALF)


def copies(count):
    return pltpu.SemaphoreType.DMA((count,))


MATRICES = scratch(4, N_SEQ, SHARD, WIDTH)
HBM = pl.BlockSpec(memory_space=pltpu.HBM)
ROOM = pltpu.CompilerParams(vmem_limit_bytes=28 << 20)


def call_project(offsets, acts, gathered):
    return pl.pallas_call(
        project,
        name="project",
        out_shape=(
            shaped(ROWS, 2 * WIDTH),
            shaped(ROWS, 2 * WIDTH),
            shaped(2 * PAIR + 16, 2 * WIDTH),
            shaped(PAIR + BLOCK + 16, 2 * WIDTH),
            MATRICES,
        ),
        in_specs=[SMEM, VMEM, HBM],
        out_specs=(VMEM,) * 5,
        scratch_shapes=[copies(4)],
        compiler_params=ROOM,
    )(offsets, *in_vmem(acts), pltpu.with_memory_space_constraint(gathered, pltpu.HBM))


def call_attend(offsets, kv, qd, prev, after, whole):
    return pl.pallas_call(
        attend,
        name="attend",
        out_shape=shaped(N_HEAD, 3, ROWS, WIDTH),
        in_specs=[SMEM] + [VMEM] * 5,
        out_specs=VMEM,
        scratch_shapes=[
            scratch(4 * PAIR, 2 * WIDTH),
            scratch(3 * PAIR + BLOCK, 2 * WIDTH),
            scratch(ROWS, WIDTH),
            scratch(ROWS, WIDTH),
            scratch(ROWS, 2 * WIDTH),
            pltpu.VMEM((4, PAIR, REACH), FONE),
        ],
        compiler_params=ROOM,
    )(offsets, *in_vmem(kv, qd, prev, after, whole))


def band_offsets(band_start, band_end, shard):
    blocks = ROWS // BLOCK
    before = shard * blocks + jnp.arange(blocks, dtype=jnp.int32) - 1
    return jnp.concatenate([band_start - before, band_end - before])


def per_device(target, source, w_query, w_key, w_value, w_out, band_start, band_end, cotangent):
    shard = lax.axis_index("seq")
    offsets = band_offsets(band_start, band_end, shard)

    w_mine = jnp.stack([w_query, w_key, w_value, w_out])
    w_z = lax.all_gather(w_mine, "seq", axis=0, axis_index_groups=Z_GROUPS)
    target, source, cotangent, w_z = lax.optimization_barrier((target, source, cotangent, w_z))
    gathered = lax.all_gather(w_z, "seq", axis=0, axis_index_groups=YC_GROUPS)
    acts = jnp.stack([target, source, cotangent])
    acts = jnp.broadcast_to(acts[None], (N_HEAD,) + acts.shape)
    acts = lax.all_to_all(acts, "head", 0, 0)
    acts, gathered, offsets = lax.optimization_barrier((acts, gathered, offsets))

    kv, qd, to_next, to_prev, whole = call_project(offsets, acts, gathered)
    prev = passed_along(to_next, "seq", 1)
    after = passed_along(to_prev, "seq", -1)
    terms = call_attend(offsets, kv, qd, prev, after, whole)
    terms = lax.all_to_all(terms, "head", 0, 0)
    return tuple(jnp.sum(terms[:, i].astype(FONE), axis=0).astype(HALF) for i in range(3))


def solution(mesh):
    sharded = P("seq", "head")
    in_specs = (sharded,) * 6 + (P("seq"), P("seq"), sharded)
    return jax.shard_map(
        per_device, mesh=mesh, in_specs=in_specs, out_specs=(sharded,) * 3, check_vma=False
    )
```

```python
import jax
import jax.numpy as jnp
from jax import lax
from jax.experimental import pallas as pl
from jax.experimental.pallas import tpu as pltpu
from jax.sharding import PartitionSpec as P

HEAD_DIM = 128
BLOCK = 64
MAXW = 3
N_Z, N_Y, N_CORE = 4, 8, 2
N_SEQ = N_Z * N_Y * N_CORE
N_HEAD = 8
ROWS = 256
WIDTH = 256
SHARD = 32
PAIR = 2 * BLOCK
REACH = 3 * PAIR
HALF = jnp.bfloat16
FONE = jnp.float32


Z_GROUPS = [
    [z * N_Y * N_CORE + k for z in range(N_Z)] for k in range(N_Y * N_CORE)
]
YC_GROUPS = [[z * N_Y * N_CORE + k for k in range(N_Y * N_CORE)] for z in range(N_Z)]


def passed_along(shard, axis, by):
    pairs = [(i, i + by) for i in range(N_SEQ) if 0 <= i + by < N_SEQ]
    return lax.ppermute(shard, axis, pairs)


def nt(left, right):
    return lax.dot_general(left, right, (((1,), (1,)), ((), ())), preferred_element_type=FONE)


def tn(left, right):
    return lax.dot_general(left, right, (((0,), (0,)), ((), ())), preferred_element_type=FONE)


def fetch_weight(gathered, weight, whole, sems):
    per = N_Y * N_CORE
    for z in range(N_Z):
        pltpu.make_async_copy(
            gathered.at[:, z, weight], whole.at[weight, pl.ds(per * z, per)], sems.at[weight]
        ).start()


def band_rows(offsets):
    row = lax.broadcasted_iota(jnp.int32, (16, 2 * WIDTH), 0)
    rows = jnp.zeros((16, 2 * WIDTH), FONE)
    for i in range(8):
        rows = jnp.where(row == i, offsets[i].astype(FONE), rows)
    return rows


def await_copies(ref, slot, sems):
    pltpu.make_async_copy(ref.at[slot], ref.at[slot], sems.at[slot]).wait()


def piece(whole, weight, head):
    per = N_SEQ // N_HEAD
    return whole[weight, per * head : per * (head + 1)].reshape(WIDTH, WIDTH)


def project(offsets, acts, gathered, kv, qd, to_next, to_prev, whole, w_sems):
    fetch_weight(gathered, 1, whole, w_sems)
    fetch_weight(gathered, 2, whole, w_sems)
    band = band_rows(offsets).astype(HALF)

    def product(which, weight, following=None):
        await_copies(whole, weight, w_sems)
        if following is not None:
            fetch_weight(gathered, following, whole, w_sems)
        parts = [
            jnp.dot(acts[head, which], piece(whole, weight, head), preferred_element_type=FONE)
            for head in range(N_HEAD)
        ]
        while len(parts) > 1:
            parts = [parts[i] + parts[i + 1] for i in range(0, len(parts), 2)]
        return parts[0].astype(HALF)

    kv[:, :WIDTH] = product(1, 1, 0)
    kv[:, WIDTH:] = product(1, 2, 3)
    qd[:, :WIDTH] = product(0, 0)
    qd[:, WIDTH:] = product(2, 3)
    to_next[:PAIR] = kv[PAIR:]
    to_next[PAIR : 2 * PAIR] = qd[PAIR:]
    to_next[2 * PAIR :] = band
    to_prev[:PAIR] = kv[:PAIR]
    to_prev[PAIR : PAIR + BLOCK] = qd[:BLOCK]
    to_prev[PAIR + BLOCK :] = band


def attend(offsets, kv, qd, prev, after, whole, terms, kvw, qdw, ctx, dq, grad, bias):
    kvw[:PAIR] = prev[:PAIR]
    kvw[PAIR : 3 * PAIR] = kv[...]
    kvw[3 * PAIR :] = after[:PAIR]
    qdw[:PAIR] = prev[PAIR : 2 * PAIR]
    qdw[PAIR : 3 * PAIR] = qd[...]
    qdw[3 * PAIR :] = after[PAIR : PAIR + BLOCK]

    own = band_rows(offsets)[:, :REACH]
    back = prev[2 * PAIR :].astype(FONE)[:, :REACH]
    ahead = after[PAIR + BLOCK :].astype(FONE)[:, :REACH]
    rows = [(back, 2), (back, 3), (own, 0), (own, 1), (own, 2), (own, 3), (ahead, 0), (ahead, 0)]
    lows = [source[i : i + 1] for source, i in rows]
    highs = [source[i + 4 : i + 5] for source, i in rows]
    lower = lax.broadcasted_iota(jnp.int32, (PAIR, REACH), 0) // BLOCK
    column = lax.broadcasted_iota(jnp.int32, (PAIR, REACH), 1) // BLOCK
    scale = HEAD_DIM**-0.5
    windows = ((0, 2 * PAIR), (0, REACH), (PAIR, REACH), (2 * PAIR, 2 * PAIR))
    for pair in range(4):
        offset = (column - lower + (1 if pair == 0 else -1)).astype(FONE)
        low = jnp.where(lower == 0, lows[2 * pair], lows[2 * pair + 1])
        high = jnp.where(lower == 0, highs[2 * pair], highs[2 * pair + 1])
        bias[pair] = jnp.where((offset >= low) & (offset < high), 0.0, -1e30)

    heads = [
        (slice(low, low + HEAD_DIM), slice(WIDTH + low, WIDTH + low + HEAD_DIM))
        for low in (0, HEAD_DIM)
    ]
    d_key = [[None, None], [None, None]]
    d_value = [[None, None], [None, None]]
    for pair, (start, span) in enumerate(windows):
        own_pair = pair in (1, 2)
        count = BLOCK if pair == 3 else PAIR
        here = slice(pair * PAIR, pair * PAIR + count)
        there = slice(start, start + span)
        parts = [part for part in range(2) if start <= (1 + part) * PAIR < start + span]
        used = slice(0, span)
        if not own_pair:
            parts = parts[:1]
            used = slice(PAIR * (1 + parts[0]) - start, PAIR * (2 + parts[0]) - start)
        scores = [nt(qdw[here, left], kvw[there, left]) for left, _ in heads]
        d_probs = [nt(qdw[here, right], kvw[there, right][used]) for _, right in heads]
        probs = []
        for score in scores:
            mask = bias[pair, :count, :span]
            score = score * scale + mask
            expo = jnp.exp(score - jnp.max(score, axis=-1, keepdims=True))
            total = jnp.sum(expo, axis=-1, keepdims=True)
            if not own_pair:
                expo = jnp.where(mask < 0.0, 0.0, expo)
            probs.append(expo * (1.0 / total))
        probs_b = [prob.astype(HALF) for prob in probs]
        contexts = [
            jnp.dot(prob_b, kvw[there, right], preferred_element_type=FONE).astype(HALF)
            for prob_b, (_, right) in zip(probs_b, heads)
        ]
        for head, (left, right) in enumerate(heads):
            query, d_context = qdw[here, left], qdw[here, right]
            for part in parts:
                at = (1 + part) * PAIR - start
                v_term = tn(probs_b[head][:, at : at + PAIR], d_context)
                last = d_value[head][part]
                d_value[head][part] = v_term if last is None else last + v_term
            delta = jnp.sum(
                d_context.astype(FONE) * contexts[head].astype(FONE), axis=-1, keepdims=True
            )
            d_score = (probs[head][:, used] * (d_probs[head] - delta) * scale).astype(HALF)
            if own_pair:
                mine_rows = slice((pair - 1) * PAIR, pair * PAIR)
                ctx[mine_rows, left] = contexts[head]
                dq[mine_rows, left] = jnp.dot(
                    d_score, kvw[there, left], preferred_element_type=FONE
                ).astype(HALF)
            for part in parts:
                at = (1 + part) * PAIR - start - used.start
                k_term = tn(d_score[:, at : at + PAIR], query)
                last = d_key[head][part]
                d_key[head][part] = k_term if last is None else last + k_term
    for head, (left, right) in enumerate(heads):
        for part in range(2):
            cut = slice(part * PAIR, (part + 1) * PAIR)
            grad[cut, left] = d_key[head][part].astype(HALF)
            grad[cut, right] = d_value[head][part].astype(HALF)
    for dest in range(N_HEAD):
        terms[dest, 0] = nt(ctx[...], piece(whole, 3, dest)).astype(HALF)
        terms[dest, 1] = nt(dq[...], piece(whole, 0, dest)).astype(HALF)
        source_term = nt(grad[:, :WIDTH], piece(whole, 1, dest))
        source_term = source_term + nt(grad[:, WIDTH:], piece(whole, 2, dest))
        terms[dest, 2] = source_term.astype(HALF)


SMEM = pl.BlockSpec(memory_space=pltpu.SMEM)
VMEM = pl.BlockSpec(memory_space=pltpu.VMEM)


def shaped(*dims):
    return pltpu.VMEM(dims, HALF)


def in_vmem(*arrays):
    return [pltpu.with_memory_space_constraint(array, pltpu.VMEM) for array in arrays]


def scratch(*dims):
    return pltpu.VMEM(dims, HALF)


def copies(count):
    return pltpu.SemaphoreType.DMA((count,))


MATRICES = scratch(4, N_SEQ, SHARD, WIDTH)
HBM = pl.BlockSpec(memory_space=pltpu.HBM)
ROOM = pltpu.CompilerParams(vmem_limit_bytes=28 << 20)


def call_project(offsets, acts, gathered):
    return pl.pallas_call(
        project,
        name="project",
        out_shape=(
            shaped(ROWS, 2 * WIDTH),
            shaped(ROWS, 2 * WIDTH),
            shaped(2 * PAIR + 16, 2 * WIDTH),
            shaped(PAIR + BLOCK + 16, 2 * WIDTH),
            MATRICES,
        ),
        in_specs=[SMEM, VMEM, HBM],
        out_specs=(VMEM,) * 5,
        scratch_shapes=[copies(4)],
        compiler_params=ROOM,
    )(offsets, *in_vmem(acts), pltpu.with_memory_space_constraint(gathered, pltpu.HBM))


def call_attend(offsets, kv, qd, prev, after, whole):
    return pl.pallas_call(
        attend,
        name="attend",
        out_shape=shaped(N_HEAD, 3, ROWS, WIDTH),
        in_specs=[SMEM] + [VMEM] * 5,
        out_specs=VMEM,
        scratch_shapes=[
            scratch(4 * PAIR, 2 * WIDTH),
            scratch(3 * PAIR + BLOCK, 2 * WIDTH),
            scratch(ROWS, WIDTH),
            scratch(ROWS, WIDTH),
            scratch(ROWS, 2 * WIDTH),
            pltpu.VMEM((4, PAIR, REACH), FONE),
        ],
        compiler_params=ROOM,
    )(offsets, *in_vmem(kv, qd, prev, after, whole))


def band_offsets(band_start, band_end, shard):
    blocks = ROWS // BLOCK
    before = shard * blocks + jnp.arange(blocks, dtype=jnp.int32) - 1
    return jnp.concatenate([band_start - before, band_end - before])


def per_device(target, source, w_query, w_key, w_value, w_out, band_start, band_end, cotangent):
    shard = lax.axis_index("seq")
    offsets = band_offsets(band_start, band_end, shard)

    w_mine = jnp.stack([w_query, w_key, w_value, w_out])
    w_z = lax.all_gather(w_mine, "seq", axis=0, axis_index_groups=Z_GROUPS)
    target, source, cotangent, w_z = lax.optimization_barrier((target, source, cotangent, w_z))
    gathered = lax.all_gather(w_z, "seq", axis=0, axis_index_groups=YC_GROUPS)
    acts = jnp.stack([target, source, cotangent])
    acts = jnp.broadcast_to(acts[None], (N_HEAD,) + acts.shape)
    acts = lax.all_to_all(acts, "head", 0, 0)
    acts, gathered, offsets = lax.optimization_barrier((acts, gathered, offsets))

    kv, qd, to_next, to_prev, whole = call_project(offsets, acts, gathered)
    prev = passed_along(to_next, "seq", 1)
    after = passed_along(to_prev, "seq", -1)
    terms = call_attend(offsets, kv, qd, prev, after, whole)
    terms = lax.all_to_all(terms, "head", 0, 0)
    return tuple(jnp.sum(terms[:, i].astype(FONE), axis=0).astype(HALF) for i in range(3))


def solution(mesh):
    sharded = P("seq", "head")
    in_specs = (sharded,) * 6 + (P("seq"), P("seq"), sharded)
    return jax.shard_map(
        per_device, mesh=mesh, in_specs=in_specs, out_specs=(sharded,) * 3, check_vma=False
    )
```

```python
import jax
import jax.numpy as jnp
from jax import lax
from jax.experimental import pallas as pl
from jax.experimental.pallas import tpu as pltpu
from jax.sharding import PartitionSpec as P

HEAD_DIM = 128
BLOCK = 64
MAXW = 3
N_Z, N_Y, N_CORE = 4, 8, 2
N_SEQ = N_Z * N_Y * N_CORE
N_HEAD = 8
ROWS = 256
WIDTH = 256
SHARD = 32
PAIR = 2 * BLOCK
REACH = 3 * PAIR
HALF = jnp.bfloat16
FONE = jnp.float32


Z_GROUPS = [
    [z * N_Y * N_CORE + k for z in range(N_Z)] for k in range(N_Y * N_CORE)
]
YC_GROUPS = [[z * N_Y * N_CORE + k for k in range(N_Y * N_CORE)] for z in range(N_Z)]


def passed_along(shard, axis, by):
    pairs = [(i, i + by) for i in range(N_SEQ) if 0 <= i + by < N_SEQ]
    return lax.ppermute(shard, axis, pairs)


def nt(left, right):
    return lax.dot_general(left, right, (((1,), (1,)), ((), ())), preferred_element_type=FONE)


def tn(left, right):
    return lax.dot_general(left, right, (((0,), (0,)), ((), ())), preferred_element_type=FONE)


def band_rows(offsets):
    row = lax.broadcasted_iota(jnp.int32, (16, 2 * WIDTH), 0)
    rows = jnp.zeros((16, 2 * WIDTH), FONE)
    for i in range(8):
        rows = jnp.where(row == i, offsets[i].astype(FONE), rows)
    return rows


def piece(whole, weight, head):
    per = N_SEQ // N_HEAD
    low = per * (head % 2)
    return whole[low : low + per, head // 2, weight].reshape(WIDTH, WIDTH)


def project(offsets, acts, gathered, kv, qd, to_next, to_prev, whole, partial, sems):
    half = N_Y * N_CORE // 2
    loads = [
        pltpu.make_async_copy(
            gathered.at[pl.ds(part * half, half)], whole.at[pl.ds(part * half, half)], sems.at[part]
        )
        for part in range(2)
    ]
    for load in loads:
        load.start()
    band = band_rows(offsets).astype(HALF)

    def product(which, weight, part):
        terms = [
            jnp.dot(acts[head, which], piece(whole, weight, head), preferred_element_type=FONE)
            for head in range(part, N_HEAD, 2)
        ]
        return (terms[0] + terms[1]) + (terms[2] + terms[3])

    jobs = ((1, 1, kv, 0), (1, 2, kv, WIDTH), (0, 0, qd, 0), (2, 3, qd, WIDTH))
    loads[0].wait()
    for which, weight, _, _ in jobs:
        partial[weight] = product(which, weight, 0)
    loads[1].wait()
    for which, weight, ref, low in jobs:
        ref[:, low : low + WIDTH] = (partial[weight] + product(which, weight, 1)).astype(HALF)
    to_next[:PAIR] = kv[PAIR:]
    to_next[PAIR : 2 * PAIR] = qd[PAIR:]
    to_next[2 * PAIR :] = band
    to_prev[:PAIR] = kv[:PAIR]
    to_prev[PAIR : PAIR + BLOCK] = qd[:BLOCK]
    to_prev[PAIR + BLOCK :] = band


def attend(offsets, kv, qd, prev, after, whole, terms, kvw, qdw, ctx, dq, grad, bias):
    kvw[:PAIR] = prev[:PAIR]
    kvw[PAIR : 3 * PAIR] = kv[...]
    kvw[3 * PAIR :] = after[:PAIR]
    qdw[:PAIR] = prev[PAIR : 2 * PAIR]
    qdw[PAIR : 3 * PAIR] = qd[...]
    qdw[3 * PAIR :] = after[PAIR : PAIR + BLOCK]

    own = band_rows(offsets)[:, :REACH]
    back = prev[2 * PAIR :].astype(FONE)[:, :REACH]
    ahead = after[PAIR + BLOCK :].astype(FONE)[:, :REACH]
    rows = [(back, 2), (back, 3), (own, 0), (own, 1), (own, 2), (own, 3), (ahead, 0), (ahead, 0)]
    lows = [source[i : i + 1] for source, i in rows]
    highs = [source[i + 4 : i + 5] for source, i in rows]
    lower = lax.broadcasted_iota(jnp.int32, (PAIR, REACH), 0) // BLOCK
    column = lax.broadcasted_iota(jnp.int32, (PAIR, REACH), 1) // BLOCK
    scale = HEAD_DIM**-0.5
    windows = ((0, 2 * PAIR), (0, REACH), (PAIR, REACH), (2 * PAIR, 2 * PAIR))
    for pair in range(4):
        offset = (column - lower + (1 if pair == 0 else -1)).astype(FONE)
        low = jnp.where(lower == 0, lows[2 * pair], lows[2 * pair + 1])
        high = jnp.where(lower == 0, highs[2 * pair], highs[2 * pair + 1])
        bias[pair] = jnp.where((offset >= low) & (offset < high), 0.0, -1e30)

    heads = [
        (slice(low, low + HEAD_DIM), slice(WIDTH + low, WIDTH + low + HEAD_DIM))
        for low in (0, HEAD_DIM)
    ]
    d_key = [[None, None], [None, None]]
    d_value = [[None, None], [None, None]]
    for pair, (start, span) in enumerate(windows):
        own_pair = pair in (1, 2)
        count = BLOCK if pair == 3 else PAIR
        here = slice(pair * PAIR, pair * PAIR + count)
        there = slice(start, start + span)
        parts = [part for part in range(2) if start <= (1 + part) * PAIR < start + span]
        used = slice(0, span)
        if not own_pair:
            parts = parts[:1]
            used = slice(PAIR * (1 + parts[0]) - start, PAIR * (2 + parts[0]) - start)
        scores = [nt(qdw[here, left], kvw[there, left]) for left, _ in heads]
        d_probs = [nt(qdw[here, right], kvw[there, right][used]) for _, right in heads]
        probs = []
        for score in scores:
            mask = bias[pair, :count, :span]
            score = score * scale + mask
            expo = jnp.exp(score - jnp.max(score, axis=-1, keepdims=True))
            total = jnp.sum(expo, axis=-1, keepdims=True)
            if not own_pair:
                expo = jnp.where(mask < 0.0, 0.0, expo)
            probs.append(expo * (1.0 / total))
        probs_b = [prob.astype(HALF) for prob in probs]
        contexts = [
            jnp.dot(prob_b, kvw[there, right], preferred_element_type=FONE).astype(HALF)
            for prob_b, (_, right) in zip(probs_b, heads)
        ]
        for head, (left, right) in enumerate(heads):
            query, d_context = qdw[here, left], qdw[here, right]
            for part in parts:
                at = (1 + part) * PAIR - start
                v_term = tn(probs_b[head][:, at : at + PAIR], d_context)
                last = d_value[head][part]
                d_value[head][part] = v_term if last is None else last + v_term
            delta = jnp.sum(
                d_context.astype(FONE) * contexts[head].astype(FONE), axis=-1, keepdims=True
            )
            d_score = (probs[head][:, used] * (d_probs[head] - delta) * scale).astype(HALF)
            if own_pair:
                mine_rows = slice((pair - 1) * PAIR, pair * PAIR)
                ctx[mine_rows, left] = contexts[head]
                dq[mine_rows, left] = jnp.dot(
                    d_score, kvw[there, left], preferred_element_type=FONE
                ).astype(HALF)
            for part in parts:
                at = (1 + part) * PAIR - start - used.start
                k_term = tn(d_score[:, at : at + PAIR], query)
                last = d_key[head][part]
                d_key[head][part] = k_term if last is None else last + k_term
    for head, (left, right) in enumerate(heads):
        for part in range(2):
            cut = slice(part * PAIR, (part + 1) * PAIR)
            grad[cut, left] = d_key[head][part].astype(HALF)
            grad[cut, right] = d_value[head][part].astype(HALF)
    for dest in range(N_HEAD):
        terms[dest, 0] = nt(ctx[...], piece(whole, 3, dest)).astype(HALF)
        terms[dest, 1] = nt(dq[...], piece(whole, 0, dest)).astype(HALF)
        source_term = nt(grad[:, :WIDTH], piece(whole, 1, dest))
        source_term = source_term + nt(grad[:, WIDTH:], piece(whole, 2, dest))
        terms[dest, 2] = source_term.astype(HALF)


SMEM = pl.BlockSpec(memory_space=pltpu.SMEM)
VMEM = pl.BlockSpec(memory_space=pltpu.VMEM)


def shaped(*dims):
    return pltpu.VMEM(dims, HALF)


def in_vmem(*arrays):
    return [pltpu.with_memory_space_constraint(array, pltpu.VMEM) for array in arrays]


def scratch(*dims):
    return pltpu.VMEM(dims, HALF)


def copies(count):
    return pltpu.SemaphoreType.DMA((count,))


MATRICES = scratch(N_Y * N_CORE, N_Z, 4, SHARD, WIDTH)
HBM = pl.BlockSpec(memory_space=pltpu.HBM)
ROOM = pltpu.CompilerParams(vmem_limit_bytes=28 << 20)


def call_project(offsets, acts, gathered):
    return pl.pallas_call(
        project,
        name="project",
        out_shape=(
            shaped(ROWS, 2 * WIDTH),
            shaped(ROWS, 2 * WIDTH),
            shaped(2 * PAIR + 16, 2 * WIDTH),
            shaped(PAIR + BLOCK + 16, 2 * WIDTH),
            MATRICES,
        ),
        in_specs=[SMEM, VMEM, HBM],
        out_specs=(VMEM,) * 5,
        scratch_shapes=[pltpu.VMEM((4, ROWS, WIDTH), FONE), copies(2)],
        compiler_params=ROOM,
    )(offsets, *in_vmem(acts), pltpu.with_memory_space_constraint(gathered, pltpu.HBM))


def call_attend(offsets, kv, qd, prev, after, whole):
    return pl.pallas_call(
        attend,
        name="attend",
        out_shape=shaped(N_HEAD, 3, ROWS, WIDTH),
        in_specs=[SMEM] + [VMEM] * 5,
        out_specs=VMEM,
        scratch_shapes=[
            scratch(4 * PAIR, 2 * WIDTH),
            scratch(3 * PAIR + BLOCK, 2 * WIDTH),
            scratch(ROWS, WIDTH),
            scratch(ROWS, WIDTH),
            scratch(ROWS, 2 * WIDTH),
            pltpu.VMEM((4, PAIR, REACH), FONE),
        ],
        compiler_params=ROOM,
    )(offsets, *in_vmem(kv, qd, prev, after, whole))


def band_offsets(band_start, band_end, shard):
    blocks = ROWS // BLOCK
    before = shard * blocks + jnp.arange(blocks, dtype=jnp.int32) - 1
    return jnp.concatenate([band_start - before, band_end - before])


def per_device(target, source, w_query, w_key, w_value, w_out, band_start, band_end, cotangent):
    shard = lax.axis_index("seq")
    offsets = band_offsets(band_start, band_end, shard)

    w_mine = jnp.stack([w_query, w_key, w_value, w_out])
    w_z = lax.all_gather(w_mine, "seq", axis=0, axis_index_groups=Z_GROUPS)
    target, source, cotangent, w_z = lax.optimization_barrier((target, source, cotangent, w_z))
    gathered = lax.all_gather(w_z, "seq", axis=0, axis_index_groups=YC_GROUPS)
    acts = jnp.stack([target, source, cotangent])
    acts = jnp.broadcast_to(acts[None], (N_HEAD,) + acts.shape)
    acts = lax.all_to_all(acts, "head", 0, 0)
    acts, gathered, offsets = lax.optimization_barrier((acts, gathered, offsets))

    kv, qd, to_next, to_prev, whole = call_project(offsets, acts, gathered)
    prev = passed_along(to_next, "seq", 1)
    after = passed_along(to_prev, "seq", -1)
    terms = call_attend(offsets, kv, qd, prev, after, whole)
    terms = lax.all_to_all(terms, "head", 0, 0)
    return tuple(jnp.sum(terms[:, i].astype(FONE), axis=0).astype(HALF) for i in range(3))


def solution(mesh):
    sharded = P("seq", "head")
    in_specs = (sharded,) * 6 + (P("seq"), P("seq"), sharded)
    return jax.shard_map(
        per_device, mesh=mesh, in_specs=in_specs, out_specs=(sharded,) * 3, check_vma=False
    )
```

```python
import jax
import jax.numpy as jnp
from jax import lax
from jax.experimental import pallas as pl
from jax.experimental.pallas import tpu as pltpu
from jax.sharding import PartitionSpec as P

HEAD_DIM = 128
BLOCK = 64
MAXW = 3
N_Z, N_Y, N_CORE = 4, 8, 2
N_SEQ = N_Z * N_Y * N_CORE
N_HEAD = 8
ROWS = 256
WIDTH = 256
SHARD = 32
PAIR = 2 * BLOCK
REACH = 3 * PAIR
HALF = jnp.bfloat16
FONE = jnp.float32


Z_GROUPS = [
    [z * N_Y * N_CORE + k for z in range(N_Z)] for k in range(N_Y * N_CORE)
]
YC_GROUPS = [[z * N_Y * N_CORE + k for k in range(N_Y * N_CORE)] for z in range(N_Z)]


def passed_along(shard, axis, by):
    pairs = [(i, i + by) for i in range(N_SEQ) if 0 <= i + by < N_SEQ]
    return lax.ppermute(shard, axis, pairs)


def nt(left, right):
    return lax.dot_general(left, right, (((1,), (1,)), ((), ())), preferred_element_type=FONE)


def tn(left, right):
    return lax.dot_general(left, right, (((0,), (0,)), ((), ())), preferred_element_type=FONE)


def band_rows(offsets):
    row = lax.broadcasted_iota(jnp.int32, (16, 2 * WIDTH), 0)
    rows = jnp.zeros((16, 2 * WIDTH), FONE)
    for i in range(8):
        rows = jnp.where(row == i, offsets[i].astype(FONE), rows)
    return rows


def piece(whole, weight, head):
    per = N_SEQ // N_HEAD
    low = per * (head % 2)
    return whole[low : low + per, head // 2, weight].reshape(WIDTH, WIDTH)


def project(offsets, acts, gathered, kv, qd, to_next, to_prev, whole, partial, sems):
    count = N_Y * N_CORE // 4
    loads = [
        pltpu.make_async_copy(
            gathered.at[pl.ds(part * count, count)], whole.at[pl.ds(part * count, count)], sems.at[part]
        )
        for part in range(4)
    ]
    for load in loads:
        load.start()
    band = band_rows(offsets).astype(HALF)

    def product(which, weight, part):
        terms = [
            jnp.dot(acts[head, which], piece(whole, weight, head), preferred_element_type=FONE)
            for head in range(part, N_HEAD, 2)
        ]
        return (terms[0] + terms[1]) + (terms[2] + terms[3])

    jobs = ((1, 1, kv, 0), (1, 2, kv, WIDTH), (0, 0, qd, 0), (2, 3, qd, WIDTH))
    loads[0].wait()
    loads[1].wait()
    for which, weight, _, _ in jobs:
        partial[weight] = product(which, weight, 0)
    loads[2].wait()
    loads[3].wait()
    for which, weight, ref, low in jobs:
        ref[:, low : low + WIDTH] = (partial[weight] + product(which, weight, 1)).astype(HALF)
    to_next[:PAIR] = kv[PAIR:]
    to_next[PAIR : 2 * PAIR] = qd[PAIR:]
    to_next[2 * PAIR :] = band
    to_prev[:PAIR] = kv[:PAIR]
    to_prev[PAIR : PAIR + BLOCK] = qd[:BLOCK]
    to_prev[PAIR + BLOCK :] = band


def attend(offsets, kv, qd, prev, after, whole, terms, kvw, qdw, ctx, dq, grad, bias):
    kvw[:PAIR] = prev[:PAIR]
    kvw[PAIR : 3 * PAIR] = kv[...]
    kvw[3 * PAIR :] = after[:PAIR]
    qdw[:PAIR] = prev[PAIR : 2 * PAIR]
    qdw[PAIR : 3 * PAIR] = qd[...]
    qdw[3 * PAIR :] = after[PAIR : PAIR + BLOCK]

    own = band_rows(offsets)[:, :REACH]
    back = prev[2 * PAIR :].astype(FONE)[:, :REACH]
    ahead = after[PAIR + BLOCK :].astype(FONE)[:, :REACH]
    rows = [(back, 2), (back, 3), (own, 0), (own, 1), (own, 2), (own, 3), (ahead, 0), (ahead, 0)]
    lows = [source[i : i + 1] for source, i in rows]
    highs = [source[i + 4 : i + 5] for source, i in rows]
    lower = lax.broadcasted_iota(jnp.int32, (PAIR, REACH), 0) // BLOCK
    column = lax.broadcasted_iota(jnp.int32, (PAIR, REACH), 1) // BLOCK
    scale = HEAD_DIM**-0.5
    windows = ((0, 2 * PAIR), (0, REACH), (PAIR, REACH), (2 * PAIR, 2 * PAIR))
    for pair in range(4):
        offset = (column - lower + (1 if pair == 0 else -1)).astype(FONE)
        low = jnp.where(lower == 0, lows[2 * pair], lows[2 * pair + 1])
        high = jnp.where(lower == 0, highs[2 * pair], highs[2 * pair + 1])
        bias[pair] = jnp.where((offset >= low) & (offset < high), 0.0, -1e30)

    heads = [
        (slice(low, low + HEAD_DIM), slice(WIDTH + low, WIDTH + low + HEAD_DIM))
        for low in (0, HEAD_DIM)
    ]
    d_key = [[None, None], [None, None]]
    d_value = [[None, None], [None, None]]
    for pair, (start, span) in enumerate(windows):
        own_pair = pair in (1, 2)
        count = BLOCK if pair == 3 else PAIR
        here = slice(pair * PAIR, pair * PAIR + count)
        there = slice(start, start + span)
        parts = [part for part in range(2) if start <= (1 + part) * PAIR < start + span]
        used = slice(0, span)
        if not own_pair:
            parts = parts[:1]
            used = slice(PAIR * (1 + parts[0]) - start, PAIR * (2 + parts[0]) - start)
        scores = [nt(qdw[here, left], kvw[there, left]) for left, _ in heads]
        d_probs = [nt(qdw[here, right], kvw[there, right][used]) for _, right in heads]
        probs = []
        for score in scores:
            mask = bias[pair, :count, :span]
            score = score * scale + mask
            expo = jnp.exp(score - jnp.max(score, axis=-1, keepdims=True))
            total = jnp.sum(expo, axis=-1, keepdims=True)
            if not own_pair:
                expo = jnp.where(mask < 0.0, 0.0, expo)
            probs.append(expo * (1.0 / total))
        probs_b = [prob.astype(HALF) for prob in probs]
        contexts = [
            jnp.dot(prob_b, kvw[there, right], preferred_element_type=FONE).astype(HALF)
            for prob_b, (_, right) in zip(probs_b, heads)
        ]
        for head, (left, right) in enumerate(heads):
            query, d_context = qdw[here, left], qdw[here, right]
            for part in parts:
                at = (1 + part) * PAIR - start
                v_term = tn(probs_b[head][:, at : at + PAIR], d_context)
                last = d_value[head][part]
                d_value[head][part] = v_term if last is None else last + v_term
            delta = jnp.sum(
                d_context.astype(FONE) * contexts[head].astype(FONE), axis=-1, keepdims=True
            )
            d_score = (probs[head][:, used] * (d_probs[head] - delta) * scale).astype(HALF)
            if own_pair:
                mine_rows = slice((pair - 1) * PAIR, pair * PAIR)
                ctx[mine_rows, left] = contexts[head]
                dq[mine_rows, left] = jnp.dot(
                    d_score, kvw[there, left], preferred_element_type=FONE
                ).astype(HALF)
            for part in parts:
                at = (1 + part) * PAIR - start - used.start
                k_term = tn(d_score[:, at : at + PAIR], query)
                last = d_key[head][part]
                d_key[head][part] = k_term if last is None else last + k_term
    for head, (left, right) in enumerate(heads):
        for part in range(2):
            cut = slice(part * PAIR, (part + 1) * PAIR)
            grad[cut, left] = d_key[head][part].astype(HALF)
            grad[cut, right] = d_value[head][part].astype(HALF)
    for dest in range(N_HEAD):
        terms[dest, 0] = nt(ctx[...], piece(whole, 3, dest)).astype(HALF)
        terms[dest, 1] = nt(dq[...], piece(whole, 0, dest)).astype(HALF)
        source_term = nt(grad[:, :WIDTH], piece(whole, 1, dest))
        source_term = source_term + nt(grad[:, WIDTH:], piece(whole, 2, dest))
        terms[dest, 2] = source_term.astype(HALF)


SMEM = pl.BlockSpec(memory_space=pltpu.SMEM)
VMEM = pl.BlockSpec(memory_space=pltpu.VMEM)


def shaped(*dims):
    return pltpu.VMEM(dims, HALF)


def in_vmem(*arrays):
    return [pltpu.with_memory_space_constraint(array, pltpu.VMEM) for array in arrays]


def scratch(*dims):
    return pltpu.VMEM(dims, HALF)


def copies(count):
    return pltpu.SemaphoreType.DMA((count,))


MATRICES = scratch(N_Y * N_CORE, N_Z, 4, SHARD, WIDTH)
HBM = pl.BlockSpec(memory_space=pltpu.HBM)
ROOM = pltpu.CompilerParams(vmem_limit_bytes=28 << 20)


def call_project(offsets, acts, gathered):
    return pl.pallas_call(
        project,
        name="project",
        out_shape=(
            shaped(ROWS, 2 * WIDTH),
            shaped(ROWS, 2 * WIDTH),
            shaped(2 * PAIR + 16, 2 * WIDTH),
            shaped(PAIR + BLOCK + 16, 2 * WIDTH),
            MATRICES,
        ),
        in_specs=[SMEM, VMEM, HBM],
        out_specs=(VMEM,) * 5,
        scratch_shapes=[pltpu.VMEM((4, ROWS, WIDTH), FONE), copies(4)],
        compiler_params=ROOM,
    )(offsets, *in_vmem(acts), pltpu.with_memory_space_constraint(gathered, pltpu.HBM))


def call_attend(offsets, kv, qd, prev, after, whole):
    return pl.pallas_call(
        attend,
        name="attend",
        out_shape=shaped(N_HEAD, 3, ROWS, WIDTH),
        in_specs=[SMEM] + [VMEM] * 5,
        out_specs=VMEM,
        scratch_shapes=[
            scratch(4 * PAIR, 2 * WIDTH),
            scratch(3 * PAIR + BLOCK, 2 * WIDTH),
            scratch(ROWS, WIDTH),
            scratch(ROWS, WIDTH),
            scratch(ROWS, 2 * WIDTH),
            pltpu.VMEM((4, PAIR, REACH), FONE),
        ],
        compiler_params=ROOM,
    )(offsets, *in_vmem(kv, qd, prev, after, whole))


def band_offsets(band_start, band_end, shard):
    blocks = ROWS // BLOCK
    before = shard * blocks + jnp.arange(blocks, dtype=jnp.int32) - 1
    return jnp.concatenate([band_start - before, band_end - before])


def per_device(target, source, w_query, w_key, w_value, w_out, band_start, band_end, cotangent):
    shard = lax.axis_index("seq")
    offsets = band_offsets(band_start, band_end, shard)

    w_mine = jnp.stack([w_query, w_key, w_value, w_out])
    w_z = lax.all_gather(w_mine, "seq", axis=0, axis_index_groups=Z_GROUPS)
    target, source, cotangent, w_z = lax.optimization_barrier((target, source, cotangent, w_z))
    gathered = lax.all_gather(w_z, "seq", axis=0, axis_index_groups=YC_GROUPS)
    acts = jnp.stack([target, source, cotangent])
    acts = jnp.broadcast_to(acts[None], (N_HEAD,) + acts.shape)
    acts = lax.all_to_all(acts, "head", 0, 0)
    acts, gathered, offsets = lax.optimization_barrier((acts, gathered, offsets))

    kv, qd, to_next, to_prev, whole = call_project(offsets, acts, gathered)
    prev = passed_along(to_next, "seq", 1)
    after = passed_along(to_prev, "seq", -1)
    terms = call_attend(offsets, kv, qd, prev, after, whole)
    terms = lax.all_to_all(terms, "head", 0, 0)
    return tuple(jnp.sum(terms[:, i].astype(FONE), axis=0).astype(HALF) for i in range(3))


def solution(mesh):
    sharded = P("seq", "head")
    in_specs = (sharded,) * 6 + (P("seq"), P("seq"), sharded)
    return jax.shard_map(
        per_device, mesh=mesh, in_specs=in_specs, out_specs=(sharded,) * 3, check_vma=False
    )
```
